128 devices in a mesh: wave: 16 (over x, y), lat: 8 (over z, core).
Axes of the slice: x: 4, y: 4, z: 4, core: 2. Of those that a mesh axis runs over, the one named last changes fastest.
Arguments:
- control: bfloat16 [320, 641, 8, 137], P('wave', None, 'lat'), may hold values from -6 to 6
- spread: float32 [4, 640, 137], replicated, may hold values from 0.3 to 3
- vertical: bfloat16 [4, 137, 137], replicated, may hold values from -0.5 to 0.5
- legendre: bfloat16 [320, 641, 512], P('wave'), may hold values from -0.0048828125 to 0.0048828125
- column_index: int32 [65536], P(('wave', 'lat')), may hold values from 0 to 10239
- column_owner: int32 [65536, 1], P(('wave', 'lat')), may hold values from 0 to 127; in each aligned block of 512 rows (0 to 511, 512 to 1023, ...) at most 8 rows name the same one
- jacobian: bfloat16 [128, 366, 548], P(('wave', 'lat')), may hold values from -0.25 to 0.25
- channel_bias: float32 [128, 366], P(('wave', 'lat')), may hold values from -5 to 5
Outputs:
- departures: bfloat16 [65536, 366], P(('wave', 'lat'))
- increments: bfloat16 [65536, 548], P(('wave', 'lat'))
The draws below stay inside these ranges and needn't reach their ends.
Inputs may be any that keep to these rules, and one draw needn't show every extreme that they name: `column_owner`: in each aligned block of 512 rows no owner appears more than 8 times, and some owner appears exactly 8 times.
All inputs are finite; a program needn't handle non-finite values.
Results may differ from the reference program's by a relative error of at most 0.0072.
Values may be sent and summed in bfloat16 or wider, within the bound.
No kernel may reach another device: no remote copies, remote signals or barrier semaphores. Data moves between devices by JAX's collectives and lax.ppermute only.
A program may use at most 128 MiB of HBM per device.

```python
import math
import jax
import jax.numpy as jnp
import numpy as np
from jax import lax

V = 4
L = 137
MMAX = 640
NLON = 2560
CH = 366
LAT_DEV = 4
COLS_DEV = 512
CAP = 8
PAIRS = 320
J = 641
VC = 8
VL = 548
NLAT = 512
COLUMNS = 65536
DEVICES = 128


def place_ends(result, own_key, low, high):
    longest = result.shape.index(max(result.shape))
    spots = []
    for shift in (0, 1):
        where = [jax.random.randint(jax.random.fold_in(own_key, axis), (), 0, length) for axis, length in enumerate(result.shape)]
        where[longest] = (where[longest] + shift) % result.shape[longest]
        spots.append(tuple(where))
    return result.at[spots[0]].set(low).at[spots[1]].set(high)


def level_of(own_key, extent, shards, low, high):
    def one(axis_at, parts):
        heights = jax.random.uniform(jax.random.fold_in(jax.random.fold_in(own_key, 6), axis_at), (parts,), jnp.float32, low / len(shards), high / len(shards))
        return jnp.repeat(jnp.exp(heights), extent[axis_at] // parts).reshape((-1,) + (1,) * (len(extent) - axis_at - 1))

    loudness = one(*shards[0])
    for cut in shards[1:]:
        loudness = loudness * one(*cut)
    return loudness


def routed_block(stream_key, own, number, rows, count, top, reach, slope):
    order = jax.random.permutation(stream_key, count)
    heavy_load, common = portions_of(count, rows * top, reach, slope, True), portions_of(count, rows * top, reach, slope, False)
    places = jnp.arange(count)

    def named(tallies, rotation):
        used = int((tallies > 0).sum())
        fixed = max(1, used // 4)
        moved = fixed + (places - fixed + rotation * (used - fixed)) % max(1, count - fixed)
        return jnp.zeros((count,), jnp.int32).at[order[jnp.where(places < fixed, places, moved)]].set(jnp.asarray(tallies, jnp.int32))

    tallies = jnp.where(number % 4 == 0, named(heavy_load, number // 4), named(common, number - number // 4 - 1))
    mixed = jax.random.permutation(jax.random.fold_in(own, 3), count)
    giver, taker = mixed[0:count // 2 * 2:2], mixed[1:count // 2 * 2:2]
    margin = jnp.minimum(tallies[giver] - 1, reach - tallies[taker]) // 2
    margin = jnp.where((giver == order[0]) | (taker == order[0]) | (tallies[taker] == 0), 0, jnp.maximum(margin, 0))
    moved = jax.random.randint(jax.random.fold_in(own, 4), (count // 2,), 0, 1 << 20) % (margin + 1)
    tallies = tallies.at[giver].add(-moved).at[taker].add(moved)
    items = jnp.searchsorted(jnp.cumsum(tallies), jnp.arange(rows * top), side="right").astype(jnp.int32)
    table = items.reshape(top, rows).T
    table = table[jax.random.permutation(jax.random.fold_in(own, 1), rows)]
    rotation = jax.random.randint(jax.random.fold_in(own, 2), (rows, 1), 0, top)
    return jnp.take_along_axis(table, (jnp.arange(top)[None, :] + rotation) % top, axis=1)


def portions_of(count, total, most, skew, full):
    weights = [(1 << 20) // math.isqrt(standing ** skew) + 1 for standing in range(1, count + 1)]
    largest = most if full else min(most, max(-(-total // count), total * weights[0] // sum(weights)))
    least = 1 if total - largest >= count - 1 else 0
    holding, spare = [largest] + [least] * (count - 1), total - largest - least * (count - 1)
    while spare > 0:
        movable = [i for i in range(1, count) if holding[i] < largest] or [i for i in range(1, count) if holding[i] < most]
        whole, remaining = sum([weights[i] for i in movable]), spare
        for i in movable:
            addition = min(most - holding[i], max(1, remaining * weights[i] // whole), spare)
            holding[i] = holding[i] + addition
            spare = spare - addition
    return np.array(holding)


def gaussian(key, dims, deviation, bound, split=(), held_as=jnp.bfloat16):
    drawn = deviation * jax.random.normal(key, dims, jnp.float32)
    if split:
        drawn = drawn * level_of(key, dims, split, -0.22, 0.18)
    return jnp.clip(drawn, -bound, bound).astype(held_as)


def setup_inputs(seed: int = 0) -> dict:
    keys = jax.random.split(jax.random.key(seed), 9)
    control = gaussian(keys[0], (PAIRS, J, VC, L), 1.0, 6.0, ((0, 16), (2, 8)))
    spread = jnp.clip(jnp.exp(jax.random.uniform(keys[1], (V, MMAX, L), jnp.float32, math.log(0.3), math.log(3.0))), 0.3, 3.0)
    vertical = gaussian(keys[2], (V, L, L), L ** -0.5, 0.5)
    legendre = gaussian(keys[3], (PAIRS, J, NLAT), (4 * J * MMAX) ** -0.5, 0.0048828125, ((0, 16),))
    column_index = place_ends(jax.random.randint(keys[4], (COLUMNS,), 0, LAT_DEV * NLON), jax.random.fold_in(keys[4], 1), 0, (LAT_DEV * NLON) - 1).astype(jnp.int32)
    column_owner_keys = jax.random.split(jax.random.fold_in(keys[5], 1), COLUMNS // COLS_DEV)
    column_owner_turns = jax.random.permutation(jax.random.fold_in(keys[5], 3), COLUMNS // COLS_DEV)
    column_owner = jax.vmap(lambda own, number: routed_block(jax.random.fold_in(keys[5], 2), own, number, COLS_DEV, DEVICES, 1, CAP, 2))(column_owner_keys, column_owner_turns).reshape((COLUMNS, 1))
    jacobian = gaussian(keys[6], (DEVICES, CH, VL), VL ** -0.5, 0.25, ((0, 128),))
    channel_bias = gaussian(keys[7], (DEVICES, CH), 1.0, 5.0, ((0, 128),), jnp.float32)
    return {"control": control, "spread": spread, "vertical": vertical, "legendre": legendre, "column_index": column_index, "column_owner": column_owner, "jacobian": jacobian, "channel_bias": channel_bias}


soft_scale = 0.25

def synth_table(longitude):
    pair_ids = jnp.arange(PAIRS, dtype=jnp.int32)
    wave_ids = jnp.stack([pair_ids, MMAX - 1 - pair_ids], axis=1)
    turn_ids = wave_ids[None, :, :] * longitude[:, None, None] % NLON
    phases = turn_ids.astype(jnp.float32) * jnp.float32(2.0 * math.pi / NLON)
    factor = jnp.where(wave_ids == 0, 1.0, 2.0).astype(jnp.float32)[None]
    cosine = factor * jnp.cos(phases)
    sine_part = -factor * jnp.sin(phases)
    return jnp.stack([cosine, sine_part], axis=1).reshape(longitude.shape[0], 4 * PAIRS).astype(jnp.bfloat16)

def slot_numbers(owner_block):
    owner_hits = (owner_block[:, None] == jnp.arange(DEVICES, dtype=jnp.int32)[None, :]).astype(jnp.int32)
    earlier = jnp.cumsum(owner_hits, axis=0, dtype=jnp.int32) - owner_hits
    return lax.optimization_barrier(jnp.sum(earlier * owner_hits, axis=1)).astype(jnp.int32)

def reference(control, spread, vertical, legendre, column_index, column_owner, jacobian, channel_bias):
    pair_ids = jnp.arange(PAIRS, dtype=jnp.int32)
    slot_ids = jnp.arange(J, dtype=jnp.int32)
    boundary = MMAX - pair_ids
    in_first = slot_ids[None, :] < boundary[:, None]
    wavenum = jnp.where(in_first, pair_ids[:, None] + slot_ids[None, :], slot_ids[None, :] - 1).astype(jnp.int32)
    var_ids = jnp.arange(VC, dtype=jnp.int32) // 2
    selected_modes = vertical[var_ids].astype(jnp.float32)

    def one_pair(members):
        control_p, wave_nums, first_p, legendre_p = members
        scaled_state = (control_p.astype(jnp.float32) * spread[var_ids[None, :], wave_nums[:, None]]).astype(jnp.bfloat16)
        spectral_coeffs = jnp.einsum('pji,jmi->pjm', scaled_state.astype(jnp.float32), selected_modes).astype(jnp.bfloat16)
        legend_f = legendre_p.astype(jnp.float32)
        spec_f = spectral_coeffs.astype(jnp.float32)
        first_sum = jnp.einsum('sn,scl->ncl', legend_f * first_p[:, None], spec_f)
        second_sum = jnp.einsum('sn,scl->ncl', legend_f * (1.0 - first_p)[:, None], spec_f)
        return jnp.stack([first_sum, second_sum], axis=0).astype(jnp.bfloat16)
    fourier = lax.map(one_pair, (control, wavenum, in_first.astype(jnp.float32), legendre))
    coeff_rows = fourier.reshape(PAIRS, 2, NLAT, V, 2, L).transpose(2, 4, 0, 1, 3, 5).reshape(NLAT, 4 * PAIRS, V * L)

    def column_block(members):
        index_block, block_id = members
        rows_here = lax.dynamic_slice_in_dim(coeff_rows, (block_id * LAT_DEV).astype(jnp.int32), LAT_DEV, 0)
        synthesis = synth_table(index_block % NLON)
        row_of = index_block // NLON
        column_state = jnp.zeros((COLS_DEV, V * L), jnp.float32)
        for local_row in range(LAT_DEV):
            row_part = jnp.dot(synthesis, rows_here[local_row], preferred_element_type=jnp.float32)
            column_state = jnp.where((row_of == local_row)[:, None], row_part, column_state)
        return column_state.astype(jnp.bfloat16)
    block_ids = jnp.arange(DEVICES, dtype=jnp.int32)
    states = lax.map(column_block, (column_index.reshape(DEVICES, COLS_DEV), block_ids))
    owners = column_owner[:, 0].reshape(DEVICES, COLS_DEV)
    slot_ids_all = jax.vmap(slot_numbers)(owners)
    sources = jnp.broadcast_to(block_ids[:, None], owners.shape)
    buffer = jnp.zeros((DEVICES, DEVICES, CAP, V * L), jnp.bfloat16).at[owners, sources, slot_ids_all].set(states)

    def serve(members):
        gathered_rows, jacobian_rows, start_index = members
        jacobian_fourier = jacobian_rows.astype(jnp.float32)
        innovation_vector = jnp.einsum('xqp,dp->xqd', gathered_rows.astype(jnp.float32), jacobian_fourier) + start_index
        weighted_innovation = (innovation_vector / jnp.sqrt(1.0 + innovation_vector * innovation_vector * soft_scale)).astype(jnp.bfloat16)
        cost_gradient = jnp.einsum('enb,bi->eni', weighted_innovation.astype(jnp.float32), jacobian_fourier).astype(jnp.bfloat16)
        return (innovation_vector.astype(jnp.bfloat16), cost_gradient)
    depart_all, gradient_all = lax.map(serve, (buffer, jacobian, channel_bias))
    departures = depart_all[owners, sources, slot_ids_all].reshape(COLUMNS, CH)
    increments = gradient_all[owners, sources, slot_ids_all].reshape(COLUMNS, V * L)
    return (departures, increments)
```

```python
import functools
import math

import jax
import jax.numpy as jnp
from jax import lax
from jax.experimental import pallas as pl
from jax.experimental.pallas import tpu as pltpu
from jax.sharding import PartitionSpec as P

NLON = 2560
LANES = 128
SLOT_LANES = 32
F32 = jnp.float32
BF16 = jnp.bfloat16


def dot(a, b):
    return jnp.dot(a, b, preferred_element_type=F32)


def fourier_kernel(
    base_ref, ctrl_ref, spread_ref, vert_ref, leg_ref, out_ref, main_s, rem_s, remt_s, tile_s
):
    slots = ctrl_ref.shape[3]
    waves = slots - 1
    modes = ctrl_ref.shape[2]
    rows = leg_ref.shape[2]
    dests = out_ref.shape[0]
    wide = spread_ref.shape[1]
    per_dest = rows // dests
    lane = lax.broadcasted_iota(jnp.int32, (1, wide), 1)
    spread = spread_ref[...]
    second_scale = pltpu.roll(spread, 1, 1)
    pair0 = base_ref[0] + pl.program_id(0) * 4
    for i in range(4):
        pair = pair0 + i
        first_scale = pltpu.roll(spread, wide - pair, 1)
        in_first = lane < waves - pair
        scale = jnp.where(in_first, first_scale, second_scale)[:, :slots]
        scaled = (ctrl_ref[i, 0].astype(F32) * scale).astype(BF16)
        spec = dot(vert_ref[...], scaled).astype(BF16)
        keep = in_first[:, :slots]
        zero = jnp.zeros_like(spec)
        first = jnp.where(keep, spec, zero)
        second = jnp.where(keep, zero, spec)
        both = jnp.concatenate([first[:, 256:], second[:, 256:]], axis=0)
        sums = dot(both, leg_ref[i, 256:, :])
        half_rows = spec.shape[0]
        parts = (sums[:half_rows] + dot(first[:, :256], leg_ref[i, :256, :]), sums[half_rows:])
        for h in range(2):
            j = 2 * i + h
            main_s[pl.ds(j, rows, stride=8), :] = jnp.transpose(parts[h][:LANES])
            rem_s[16 * j : 16 * j + 16, :] = parts[h][LANES:]
    remt_s[...] = jnp.transpose(rem_s[...])
    rem_rows = [remt_s[pl.ds(r, dests, stride=per_dest), :] for r in range(per_dest)]
    tile_lane = lax.broadcasted_iota(jnp.int32, (1, LANES), 1) // SLOT_LANES
    for j in range(8):
        tile = jnp.zeros((dests, LANES), F32)
        for r in range(per_dest):
            moved = pltpu.roll(rem_rows[r], (SLOT_LANES * r - 16 * j) % LANES, 1)
            tile = jnp.where(tile_lane == r, moved, tile)
        tile_s[pl.ds(j, dests, stride=8), :] = tile
    main = main_s[...].reshape(dests, per_dest, 8, LANES)
    for r in range(per_dest):
        out_ref[:, :, r * LANES : (r + 1) * LANES] = main[:, r].astype(BF16)
    out_ref[:, :, per_dest * LANES :] = tile_s[...].reshape(dests, 8, LANES).astype(BF16)


def fourier_blocks(control, spread, vertical, legendre, pair_base, dests):
    pairs, slots, _, modes = control.shape
    rows = legendre.shape[2]
    ctrl = jnp.transpose(control, (0, 2, 3, 1))
    wide = -(-slots // LANES) * LANES
    spread_t = jnp.pad(jnp.transpose(spread), ((0, 0), (0, wide - spread.shape[0])))
    vert = jnp.pad(vertical, ((0, 144 - vertical.shape[0]), (0, 0)))
    lanes = (rows // dests + 1) * LANES
    return pl.pallas_call(
        fourier_kernel,
        out_shape=jax.ShapeDtypeStruct((dests, 2 * pairs, lanes), BF16),
        grid=(pairs // 4,),
        in_specs=[
            pl.BlockSpec(memory_space=pltpu.SMEM),
            pl.BlockSpec((4, 1, modes, slots), lambda g: (g, 0, 0, 0)),
            pl.BlockSpec((modes, wide), lambda g: (0, 0)),
            pl.BlockSpec((144, modes), lambda g: (0, 0)),
            pl.BlockSpec((4, slots, rows), lambda g: (g, 0, 0)),
        ],
        out_specs=pl.BlockSpec((dests, 8, lanes), lambda g: (0, g, 0)),
        scratch_shapes=[
            pltpu.VMEM((rows * 8, LANES), F32),
            pltpu.VMEM((LANES, rows), F32),
            pltpu.VMEM((rows, LANES), F32),
            pltpu.VMEM((dests * 8, LANES), F32),
        ],
        name="fourier",
    )(pair_base, ctrl, spread_t, vert, legendre)


def cosine(turns):
    x = turns * math.pi
    y = x * x
    s = -1.0 / 39916800.0
    for c in (1.0 / 362880.0, -1.0 / 5040.0, 1.0 / 120.0, -1.0 / 6.0, 1.0):
        s = s * y + c
    s = s * x
    return 1.0 - 2.0 * (s * s)


def state_kernel(index_ref, owner_ref, coeff_ref, out_ref, spot_ref, table_s, row_s, state_s):
    v = pl.program_id(0)
    cols = table_s.shape[0]
    depth = table_s.shape[1]
    waves = depth // 2
    slots = out_ref.shape[0] // LANES
    sources = coeff_ref.shape[0]
    per_source = waves // sources

    @pl.when(v == 0)
    def _():
        column = jnp.transpose(jnp.broadcast_to(index_ref[...].astype(F32), (LANES, cols)))[:, :1]
        row = jnp.floor((column + 0.5) * (1.0 / NLON))
        longitude = column - row * NLON
        row_s[...] = jnp.broadcast_to(row, row_s.shape)
        lane = lax.broadcasted_iota(jnp.int32, (1, depth), 1)
        source = lane // (2 * per_source)
        inner = lane - source * (2 * per_source)
        part = inner // per_source
        local = inner - part * per_source
        pair = source * (per_source // 2) + local // 2
        wave = jnp.where(local % 2 == 0, pair, waves - 1 - pair)
        weight = jnp.where(wave == 0, 1.0, 2.0).astype(F32)
        wave_f = wave.astype(F32)
        shift = part.astype(F32) * (NLON // 4)
        for c in range(0, cols, 64):
            turns = longitude[c : c + 64] * wave_f + shift
            turns = turns - jnp.floor(turns * (1.0 / NLON) + 0.5) * NLON
            table_s[c : c + 64, :] = (weight * cosine(turns * (1.0 / NLON))).astype(BF16)

    block = coeff_ref[...]
    products = dot(table_s[...], block.reshape(depth, block.shape[2]))
    row = row_s[...]
    main = jnp.zeros((cols, LANES), F32)
    rest = jnp.zeros((cols, LANES), F32)
    last = products[:, 4 * LANES :]
    for r in range(4):
        main = jnp.where(row == r, products[:, r * LANES : (r + 1) * LANES], main)
        moved = last if r == 0 else pltpu.roll(last, LANES - SLOT_LANES * r, 1)
        rest = jnp.where(row == r, moved, rest)
    state_s[v] = main.astype(BF16)
    state_s[4 + v] = rest.astype(BF16)

    @pl.when(v == pl.num_programs(0) - 1)
    def _():
        hits = lax.broadcasted_iota(jnp.int32, (LANES, cols), 0) == owner_ref[...]
        hits_f = jnp.where(hits, 1.0, 0.0).astype(F32)
        before = (
            lax.broadcasted_iota(jnp.int32, (cols, cols), 0)
            < lax.broadcasted_iota(jnp.int32, (cols, cols), 1)
        )
        earlier = dot(hits_f.astype(BF16), jnp.where(before, 1.0, 0.0).astype(BF16))
        first = (lax.broadcasted_iota(jnp.int32, (LANES, cols), 0) * slots).astype(F32)
        spot = jnp.sum(hits_f * (first + earlier), axis=0, keepdims=True).astype(jnp.int32)
        spot_ref[...] = spot
        place = lax.broadcasted_iota(jnp.int32, (slots * LANES, cols), 0) == spot
        place = jnp.where(place, 1.0, 0.0).astype(BF16)
        lane = lax.broadcasted_iota(jnp.int32, (1, LANES), 1)
        tail = jnp.zeros((cols, LANES), F32)
        for u in range(4):
            out_ref[:, u * LANES : (u + 1) * LANES] = dot(place, state_s[u]).astype(BF16)
            part = state_s[4 + u].astype(F32)
            part = part if u == 0 else pltpu.roll(part, SLOT_LANES * u, 1)
            tail = jnp.where(lane // SLOT_LANES == u, part, tail)
        out_ref[:, 4 * LANES :] = dot(place, tail.astype(BF16)).astype(BF16)


def column_states(coeff, index, owner, slots):
    sources, rows, lanes = coeff.shape
    cols = index.shape[1]
    total = slots * LANES
    return pl.pallas_call(
        state_kernel,
        out_shape=(
            jax.ShapeDtypeStruct((total, lanes), BF16),
            jax.ShapeDtypeStruct((1, cols), jnp.int32),
        ),
        grid=(4,),
        in_specs=[
            pl.BlockSpec((1, cols), lambda v: (0, 0)),
            pl.BlockSpec((1, cols), lambda v: (0, 0)),
            pl.BlockSpec((sources, rows // 4, lanes), lambda v: (0, v, 0)),
        ],
        out_specs=(
            pl.BlockSpec((total, lanes), lambda v: (0, 0)),
            pl.BlockSpec((1, cols), lambda v: (0, 0)),
        ),
        scratch_shapes=[
            pltpu.VMEM((cols, sources * rows // 4), BF16),
            pltpu.VMEM((cols, LANES), F32),
            pltpu.VMEM((8, cols, LANES), BF16),
        ],
        name="states",
    )(index, owner, coeff)


def answer_kernel(state_ref, jac_ref, bias_ref, out_ref, jac_s):
    channels = jac_ref.shape[1]
    levels = jac_ref.shape[0] // 4
    rest = levels - LANES

    @pl.when(pl.program_id(0) == 0)
    def _():
        jac = jac_ref[...].astype(F32)
        jac_s[...] = jnp.zeros_like(jac_s)
        for v in range(4):
            at = v * levels
            jac_s[v * LANES : (v + 1) * LANES, :] = jac[at : at + LANES].astype(BF16)
            lo = 4 * LANES + v * SLOT_LANES
            piece = jnp.concatenate(
                [jac[at + LANES : at + levels], jnp.zeros((16 - rest, channels), F32)], axis=0
            )
            jac_s[lo : lo + 16, :] = piece.astype(BF16)

    depart = dot(state_ref[...], jac_s[...]) + bias_ref[...]
    weighted = (depart / jnp.sqrt(1.0 + depart * depart * 0.25)).astype(BF16)
    out_ref[:, :channels] = depart.astype(BF16)
    out_ref[:, 3 * LANES : 3 * LANES + jac_ref.shape[0]] = lax.dot_general(
        weighted, jac_ref[...], (((1,), (1,)), ((), ())), preferred_element_type=F32
    ).astype(BF16)


def answers(states, jac_t, bias):
    total, lanes = states.shape
    width, channels = jac_t.shape
    out_lanes = -(-channels // LANES) * LANES + -(-width // LANES) * LANES
    steps = 2
    return pl.pallas_call(
        answer_kernel,
        out_shape=jax.ShapeDtypeStruct((total, out_lanes), BF16),
        grid=(steps,),
        in_specs=[
            pl.BlockSpec((total // steps, lanes), lambda g: (g, 0)),
            pl.BlockSpec((width, channels), lambda g: (0, 0)),
            pl.BlockSpec((1, channels), lambda g: (0, 0)),
        ],
        out_specs=pl.BlockSpec((total // steps, out_lanes), lambda g: (g, 0)),
        scratch_shapes=[pltpu.VMEM((lanes, channels), BF16)],
        name="answers",
    )(states, jac_t, bias)


def collect_kernel(spot_ref, back_ref, depart_ref, grad_ref):
    cols = spot_ref.shape[1]
    total = back_ref.shape[0]
    spot = jnp.transpose(jnp.broadcast_to(spot_ref[...].astype(F32), (LANES, cols)))[:, :1]
    place = lax.broadcasted_iota(jnp.int32, (cols, total), 1) == spot.astype(jnp.int32)
    place = jnp.where(place, 1.0, 0.0).astype(BF16)
    channels = depart_ref.shape[0]
    width = grad_ref.shape[0]
    depart = jnp.transpose(dot(place, back_ref[:, : 3 * LANES]))
    depart_ref[...] = depart[:channels].astype(BF16)
    grad = jnp.transpose(dot(place, back_ref[:, 3 * LANES :]))
    grad_ref[...] = grad[:width].astype(BF16)


def collect(spot, back, channels, width):
    cols = spot.shape[1]
    return pl.pallas_call(
        collect_kernel,
        out_shape=(
            jax.ShapeDtypeStruct((channels, cols), BF16),
            jax.ShapeDtypeStruct((width, cols), BF16),
        ),
        name="collect",
    )(spot, back)


def exchange(x):
    return lax.all_to_all(x, ("wave", "lat"), split_axis=0, concat_axis=0, tiled=True)


def local(control, spread, vertical, legendre, column_index, column_owner, jacobian, channel_bias):
    pairs = control.shape[0]
    wave_count = lax.axis_size("wave")
    device_count = wave_count * lax.axis_size("lat")
    cols = column_index.shape[0]
    slots = max(2, 2 * cols // device_count)
    var = lax.axis_index("lat") // 2
    pair_base = (lax.axis_index("wave") * pairs).astype(jnp.int32).reshape(1)
    blocks = fourier_blocks(control, spread[var], vertical[var], legendre, pair_base, device_count)
    coeff = exchange(blocks)
    coeff = coeff.reshape(wave_count, -1, coeff.shape[2])
    outgoing, spot = column_states(
        coeff, column_index.reshape(1, cols), column_owner.reshape(1, cols), slots
    )
    lanes = outgoing.shape[1]
    states = exchange(outgoing.reshape(device_count, slots, lanes))
    jac_t = jnp.transpose(jacobian[0])
    reply = answers(states.reshape(device_count * slots, lanes), jac_t, channel_bias)
    back = exchange(reply.reshape(device_count, slots, reply.shape[1]))
    departures, increments = collect(
        spot, back.reshape(device_count * slots, -1), jac_t.shape[1], jac_t.shape[0]
    )
    return (jnp.transpose(departures), jnp.transpose(increments))


def solution(mesh):
    return jax.shard_map(
        local,
        mesh=mesh,
        in_specs=(
            P("wave", None, "lat", None),
            P(),
            P(),
            P("wave", None, None),
            P(("wave", "lat")),
            P(("wave", "lat"), None),
            P(("wave", "lat"), None, None),
            P(("wave", "lat"), None),
        ),
        out_specs=(P(("wave", "lat"), None), P(("wave", "lat"), None)),
        check_vma=False,
    )
```

```python
import functools
import math

import jax
import jax.numpy as jnp
from jax import lax
from jax.experimental import pallas as pl
from jax.experimental.pallas import tpu as pltpu
from jax.sharding import PartitionSpec as P

NLON = 2560
LANES = 128
SLOT_LANES = 32
REST = 12
GROUP = 10
F32 = jnp.float32
BF16 = jnp.bfloat16


def dot(a, b):
    return jnp.dot(a, b, preferred_element_type=F32)


def fourier_kernel(base_ref, ctrl_ref, spread_ref, vert_ref, leg_ref, out_ref, main_s, rem_s):
    slots = ctrl_ref.shape[3]
    waves = slots - 1
    rows = leg_ref.shape[2]
    dests = out_ref.shape[0]
    steps = pl.num_programs(0) - 1
    g = pl.program_id(0)

    @pl.when(g == 0)
    def _():
        rem_s[...] = jnp.zeros_like(rem_s)

    @pl.when(g < steps)
    def _():
        spread = spread_ref[...]
        lane = lax.broadcasted_iota(jnp.int32, (1, waves), 1)
        slot = lax.broadcasted_iota(jnp.int32, (1, slots), 1)
        second_scale = pltpu.roll(spread, 1, 1)
        pair0 = base_ref[0] + g * 4
        rests = []
        for i in range(4):
            pair = pair0 + i
            first_scale = pltpu.roll(spread, waves - pair, 1)
            scale = jnp.where(lane < waves - pair, first_scale, second_scale)
            scale = jnp.concatenate([scale, spread[:, waves - 1 :]], axis=1)
            scaled = (ctrl_ref[i, 0].astype(F32) * scale).astype(BF16)
            spec = dot(vert_ref[...], scaled).astype(BF16)
            keep = slot < waves - pair
            zero = jnp.zeros_like(spec)
            first = jnp.where(keep, spec, zero)
            second = jnp.where(keep, zero, spec)
            both = jnp.concatenate([first[:, 256:], second[:, 256:]], axis=0)
            sums = dot(both, leg_ref[i, 256:, :])
            half_rows = spec.shape[0]
            parts = (sums[:half_rows] + dot(first[:, :256], leg_ref[i, :256, :]), sums[half_rows:])
            for h in range(2):
                j = 2 * i + h
                main_s[pl.ds(j, rows, stride=8), :] = jnp.transpose(parts[h][:LANES])
                rests.append(parts[h][LANES : LANES + REST])
        out_ref[...] = main_s[...].reshape(dests, 32, LANES).astype(BF16)
        for step in range(5):

            @pl.when(g == step)
            def _():
                for j in range(8):
                    k = 8 * step + j
                    at = LANES * (k // GROUP) + REST * (k % GROUP)
                    rem_s[at : at + REST, :] = rests[j]

    @pl.when(g == steps)
    def _():
        for u in range(4):
            main_s[pl.ds(u, rows, stride=4), :] = jnp.transpose(rem_s[u * LANES : (u + 1) * LANES])
        out_ref[:, :16, :] = main_s[: 4 * rows, :].reshape(dests, 16, LANES).astype(BF16)


def fourier_blocks(control, spread, vertical, legendre, pair_base, dests):
    pairs, slots, _, modes = control.shape
    rows = legendre.shape[2]
    ctrl = jnp.transpose(control, (0, 2, 3, 1))
    vert = jnp.pad(vertical, ((0, 144 - vertical.shape[0]), (0, 0)))
    steps = pairs // 4
    return pl.pallas_call(
        fourier_kernel,
        out_shape=jax.ShapeDtypeStruct((dests, 32 * steps + 16, LANES), BF16),
        grid=(steps + 1,),
        in_specs=[
            pl.BlockSpec(memory_space=pltpu.SMEM),
            pl.BlockSpec((4, 1, modes, slots), lambda g: (jnp.minimum(g, steps - 1), 0, 0, 0)),
            pl.BlockSpec((modes, slots - 1), lambda g: (0, 0)),
            pl.BlockSpec((144, modes), lambda g: (0, 0)),
            pl.BlockSpec((4, slots, rows), lambda g: (jnp.minimum(g, steps - 1), 0, 0)),
        ],
        out_specs=pl.BlockSpec((dests, 32, LANES), lambda g: (0, g, 0)),
        scratch_shapes=[pltpu.VMEM((rows * 8, LANES), F32), pltpu.VMEM((4 * LANES, rows), F32)],
        name="fourier",
    )(pair_base, ctrl, jnp.transpose(spread), vert, legendre)


def cosine(turns):
    x = turns * math.pi
    y = x * x
    s = -1.0 / 39916800.0
    for c in (1.0 / 362880.0, -1.0 / 5040.0, 1.0 / 120.0, -1.0 / 6.0, 1.0):
        s = s * y + c
    s = s * x
    return 1.0 - 2.0 * (s * s)


def table_kernel(index_ref, owner_ref, main_ref, rest_ref, place_ref, row_ref, spot_ref):
    cols = index_ref.shape[1]
    depth = main_ref.shape[1]
    waves = depth // 2
    slots = place_ref.shape[0] // LANES
    column = jnp.transpose(jnp.broadcast_to(index_ref[...].astype(F32), (LANES, cols)))[:, :1]
    row = jnp.floor((column + 0.5) * (1.0 / NLON))
    longitude = column - row * NLON
    row_ref[...] = jnp.broadcast_to(row, row_ref.shape)
    lane = lax.broadcasted_iota(jnp.int32, (1, depth), 1)

    def fill(ref, source, part, local):
        pair = source * 20 + local // 2
        wave = jnp.where(local % 2 == 0, pair, waves - 1 - pair)
        weight = jnp.where(wave == 0, 1.0, 2.0).astype(F32)
        wave_f = wave.astype(F32)
        shift = part.astype(F32) * (NLON // 4)
        for c in range(0, cols, 64):
            turns = longitude[c : c + 64] * wave_f + shift
            turns = turns - jnp.floor(turns * (1.0 / NLON) + 0.5) * NLON
            ref[c : c + 64, :] = (weight * cosine(turns * (1.0 / NLON))).astype(BF16)

    inner = lane % 80
    fill(main_ref, lane // 80, inner // 40, inner % 40)
    inner = lane % 128
    fill(rest_ref, inner % 32 // 2, inner % 2, inner // 32 * GROUP + lane // 128)

    hits = lax.broadcasted_iota(jnp.int32, (LANES, cols), 0) == owner_ref[...]
    hits_f = jnp.where(hits, 1.0, 0.0).astype(F32)
    before = (
        lax.broadcasted_iota(jnp.int32, (cols, cols), 0)
        < lax.broadcasted_iota(jnp.int32, (cols, cols), 1)
    )
    earlier = dot(hits_f.astype(BF16), jnp.where(before, 1.0, 0.0).astype(BF16))
    first = (lax.broadcasted_iota(jnp.int32, (LANES, cols), 0) * slots).astype(F32)
    spot = jnp.sum(hits_f * (first + earlier), axis=0, keepdims=True).astype(jnp.int32)
    spot_ref[...] = spot
    place = lax.broadcasted_iota(jnp.int32, (slots * LANES, cols), 0) == spot
    place_ref[...] = jnp.where(place, 1.0, 0.0).astype(BF16)


def tables(index, owner, depth, slots):
    cols = index.shape[1]
    return pl.pallas_call(
        table_kernel,
        out_shape=(
            jax.ShapeDtypeStruct((cols, depth), BF16),
            jax.ShapeDtypeStruct((cols, depth), BF16),
            jax.ShapeDtypeStruct((slots * LANES, cols), BF16),
            jax.ShapeDtypeStruct((cols, LANES), F32),
            jax.ShapeDtypeStruct((1, cols), jnp.int32),
        ),
        cost_estimate=pl.CostEstimate(
            flops=60 * cols * depth, bytes_accessed=4 << 20, transcendentals=0
        ),
        name="tables",
    )(index, owner)


def state_kernel(
    main_ref, rest_ref, place_ref, row_ref, coeff_ref, out_ref, coeff_s, tail_s, take_s, state_s
):
    v = pl.program_id(0)
    cols = main_ref.shape[0]
    depth = main_ref.shape[1]
    sources = coeff_ref.shape[0]
    block = coeff_ref[...].astype(F32).reshape(sources * 2, 22, 8, LANES)
    for r in range(4):
        picked = jnp.stack([block[:, 4 * g + r] for g in range(5)], axis=1)
        coeff_s[:, r * LANES : (r + 1) * LANES] = picked.reshape(depth, LANES).astype(BF16)
    take_s[...] = block[:, 20:].reshape(sources * 2 * 16, LANES)
    lane = lax.broadcasted_iota(jnp.int32, (1, LANES), 1)
    odd = v % 2
    tile = v // 2
    for u in range(4):
        picked = [take_s[pl.ds(4 * r + u, sources * 2, stride=16), :] for r in range(4)]
        for k in range(GROUP):
            at = (k * 4 + u) * sources * 2
            kept = tail_s[tile, at : at + sources * 2, :]
            for r in range(4):
                moved = pltpu.roll(picked[r], (64 * odd + 16 * r - REST * k + LANES) % LANES, 1)
                kept = jnp.where(lane // 16 == 4 * odd + r, moved, kept)
            tail_s[tile, at : at + sources * 2, :] = kept
    row = row_ref[...]
    products = dot(main_ref[...], coeff_s[...])
    main = products[:, :LANES]
    for r in range(1, 4):
        main = jnp.where(row == r, products[:, r * LANES : (r + 1) * LANES], main)
    state_s[v] = main.astype(BF16)

    @pl.when(v == pl.num_programs(0) - 1)
    def _():
        place = place_ref[...]
        tail = jnp.zeros((cols, LANES), F32)
        for half in range(2):
            products = dot(rest_ref[...], tail_s[half].astype(BF16))
            for slot in range(8):
                u = 2 * half + slot // 4
                shift = (SLOT_LANES * u - 16 * slot) % LANES
                moved = products if shift == 0 else pltpu.roll(products, shift, 1)
                hit = (row == slot % 4) & (lane // SLOT_LANES == u) & (lane % SLOT_LANES < 9)
                tail = jnp.where(hit, moved, tail)
        for u in range(4):
            out_ref[:, u * LANES : (u + 1) * LANES] = dot(place, state_s[u]).astype(BF16)
        out_ref[:, 4 * LANES :] = dot(place, tail.astype(BF16)).astype(BF16)


def column_states(coeff, main_table, rest_table, place, row):
    sources, rows, _ = coeff.shape
    cols, depth = main_table.shape
    total = place.shape[0]
    whole = lambda x: pl.BlockSpec(x.shape, lambda v: (0,) * x.ndim)
    return pl.pallas_call(
        state_kernel,
        out_shape=jax.ShapeDtypeStruct((total, 5 * LANES), BF16),
        grid=(4,),
        in_specs=[
            whole(main_table),
            whole(rest_table),
            whole(place),
            whole(row),
            pl.BlockSpec((sources, rows // 4, LANES), lambda v: (0, v, 0)),
        ],
        out_specs=pl.BlockSpec((total, 5 * LANES), lambda v: (0, 0)),
        scratch_shapes=[
            pltpu.VMEM((depth, 4 * LANES), BF16),
            pltpu.VMEM((2, depth, LANES), F32),
            pltpu.VMEM((sources * 2 * 16, LANES), F32),
            pltpu.VMEM((4, cols, LANES), BF16),
        ],
        name="states",
    )(main_table, rest_table, place, row, coeff)


def answer_kernel(state_ref, jac_ref, bias_ref, out_ref, jac_s):
    channels = jac_ref.shape[1]
    levels = jac_ref.shape[0] // 4
    rest = levels - LANES

    @pl.when(pl.program_id(0) == 0)
    def _():
        jac = jac_ref[...].astype(F32)
        jac_s[...] = jnp.zeros_like(jac_s)
        for v in range(4):
            at = v * levels
            jac_s[v * LANES : (v + 1) * LANES, :] = jac[at : at + LANES].astype(BF16)
            lo = 4 * LANES + v * SLOT_LANES
            piece = jnp.concatenate(
                [jac[at + LANES : at + levels], jnp.zeros((16 - rest, channels), F32)], axis=0
            )
            jac_s[lo : lo + 16, :] = piece.astype(BF16)

    depart = dot(state_ref[...], jac_s[...]) + bias_ref[...]
    weighted = (depart / jnp.sqrt(1.0 + depart * depart * 0.25)).astype(BF16)
    out_ref[:, :channels] = depart.astype(BF16)
    out_ref[:, 3 * LANES : 3 * LANES + jac_ref.shape[0]] = lax.dot_general(
        weighted, jac_ref[...], (((1,), (1,)), ((), ())), preferred_element_type=F32
    ).astype(BF16)


def answers(states, jac_t, bias):
    total, lanes = states.shape
    width, channels = jac_t.shape
    out_lanes = -(-channels // LANES) * LANES + -(-width // LANES) * LANES
    steps = 2
    return pl.pallas_call(
        answer_kernel,
        out_shape=jax.ShapeDtypeStruct((total, out_lanes), BF16),
        grid=(steps,),
        in_specs=[
            pl.BlockSpec((total // steps, lanes), lambda g: (g, 0)),
            pl.BlockSpec((width, channels), lambda g: (0, 0)),
            pl.BlockSpec((1, channels), lambda g: (0, 0)),
        ],
        out_specs=pl.BlockSpec((total // steps, out_lanes), lambda g: (g, 0)),
        scratch_shapes=[pltpu.VMEM((lanes, channels), BF16)],
        name="answers",
    )(states, jac_t, bias)


def collect_kernel(spot_ref, back_ref, depart_ref, grad_ref):
    cols = spot_ref.shape[1]
    total = back_ref.shape[0]
    spot = jnp.transpose(jnp.broadcast_to(spot_ref[...].astype(F32), (LANES, cols)))[:, :1]
    place = lax.broadcasted_iota(jnp.int32, (cols, total), 1) == spot.astype(jnp.int32)
    place = jnp.where(place, 1.0, 0.0).astype(BF16)
    channels = depart_ref.shape[0]
    width = grad_ref.shape[0]
    depart = jnp.transpose(dot(place, back_ref[:, : 3 * LANES]))
    depart_ref[...] = depart[:channels].astype(BF16)
    grad = jnp.transpose(dot(place, back_ref[:, 3 * LANES :]))
    grad_ref[...] = grad[:width].astype(BF16)


def collect(spot, back, channels, width):
    cols = spot.shape[1]
    return pl.pallas_call(
        collect_kernel,
        out_shape=(
            jax.ShapeDtypeStruct((channels, cols), BF16),
            jax.ShapeDtypeStruct((width, cols), BF16),
        ),
        name="collect",
    )(spot, back)


def exchange(x):
    return lax.all_to_all(x, ("wave", "lat"), split_axis=0, concat_axis=0, tiled=True)


def local(control, spread, vertical, legendre, column_index, column_owner, jacobian, channel_bias):
    pairs = control.shape[0]
    wave_count = lax.axis_size("wave")
    device_count = wave_count * lax.axis_size("lat")
    cols = column_index.shape[0]
    slots = max(2, 2 * cols // device_count)
    var = lax.axis_index("lat") // 2
    pair_base = (lax.axis_index("wave") * pairs).astype(jnp.int32).reshape(1)
    blocks = fourier_blocks(control, spread[var], vertical[var], legendre, pair_base, device_count)
    main_table, rest_table, place, row, spot = tables(
        column_index.reshape(1, cols), column_owner.reshape(1, cols), 4 * pairs * wave_count, slots
    )
    coeff = exchange(blocks).reshape(wave_count, -1, LANES)
    outgoing = column_states(coeff, main_table, rest_table, place, row)
    lanes = outgoing.shape[1]
    states = exchange(outgoing.reshape(device_count, slots, lanes))
    jac_t = jnp.transpose(jacobian[0])
    reply = answers(states.reshape(device_count * slots, lanes), jac_t, channel_bias)
    back = exchange(reply.reshape(device_count, slots, reply.shape[1]))
    departures, increments = collect(
        spot, back.reshape(device_count * slots, -1), jac_t.shape[1], jac_t.shape[0]
    )
    return (jnp.transpose(departures), jnp.transpose(increments))


def solution(mesh):
    return jax.shard_map(
        local,
        mesh=mesh,
        in_specs=(
            P("wave", None, "lat", None),
            P(),
            P(),
            P("wave", None, None),
            P(("wave", "lat")),
            P(("wave", "lat"), None),
            P(("wave", "lat"), None, None),
            P(("wave", "lat"), None),
        ),
        out_specs=(P(("wave", "lat"), None), P(("wave", "lat"), None)),
        check_vma=False,
    )
```

```python
import functools
import math

import jax
import jax.numpy as jnp
from jax import lax
from jax.experimental import pallas as pl
from jax.experimental.pallas import tpu as pltpu
from jax.sharding import PartitionSpec as P

NLON = 2560
LANES = 128
SLOT_LANES = 32
REST = 12
GROUP = 10
F32 = jnp.float32
BF16 = jnp.bfloat16


def dot(a, b):
    return jnp.dot(a, b, preferred_element_type=F32)


def fourier_kernel(base_ref, ctrl_ref, spread_ref, vert_ref, leg_ref, out_ref, main_s, rem_s):
    slots = ctrl_ref.shape[3]
    waves = slots - 1
    rows = leg_ref.shape[2]
    dests = out_ref.shape[0]
    steps = pl.num_programs(0) - 1
    g = pl.program_id(0)

    @pl.when(g == 0)
    def _():
        rem_s[...] = jnp.zeros_like(rem_s)

    @pl.when(g < steps)
    def _():
        spread = spread_ref[...]
        lane = lax.broadcasted_iota(jnp.int32, (1, waves), 1)
        slot = lax.broadcasted_iota(jnp.int32, (1, slots), 1)
        second_scale = pltpu.roll(spread, 1, 1)
        pair0 = base_ref[0] + g * 4
        rests = []
        for i in range(4):
            pair = pair0 + i
            first_scale = pltpu.roll(spread, waves - pair, 1)
            scale = jnp.where(lane < waves - pair, first_scale, second_scale)
            scale = jnp.concatenate([scale, spread[:, waves - 1 :]], axis=1)
            scaled = (ctrl_ref[i, 0].astype(F32) * scale).astype(BF16)
            spec = dot(vert_ref[...], scaled).astype(BF16)
            keep = slot < waves - pair
            zero = jnp.zeros_like(spec)
            first = jnp.where(keep, spec, zero)
            second = jnp.where(keep, zero, spec)
            both = jnp.concatenate([first[:, 256:], second[:, 256:]], axis=0)
            sums = dot(both, leg_ref[i, 256:, :])
            half_rows = spec.shape[0]
            parts = (sums[:half_rows] + dot(first[:, :256], leg_ref[i, :256, :]), sums[half_rows:])
            for h in range(2):
                j = 2 * i + h
                main_s[pl.ds(j, rows, stride=8), :] = jnp.transpose(parts[h][:LANES])
                rests.append(parts[h][LANES : LANES + REST])
        out_ref[...] = main_s[...].reshape(dests, 32, LANES).astype(BF16)
        for step in range(5):

            @pl.when(g == step)
            def _():
                for j in range(8):
                    k = 8 * step + j
                    at = LANES * (k // GROUP) + REST * (k % GROUP)
                    rem_s[at : at + REST, :] = rests[j]

    @pl.when(g == steps)
    def _():
        for u in range(4):
            main_s[pl.ds(u, rows, stride=4), :] = jnp.transpose(rem_s[u * LANES : (u + 1) * LANES])
        out_ref[:, :16, :] = main_s[: 4 * rows, :].reshape(dests, 16, LANES).astype(BF16)


def fourier_blocks(control, spread, vertical, legendre, pair_base, dests):
    pairs, slots, _, modes = control.shape
    rows = legendre.shape[2]
    ctrl = jnp.transpose(control, (0, 2, 3, 1))
    vert = jnp.pad(vertical, ((0, 144 - vertical.shape[0]), (0, 0)))
    steps = pairs // 4
    return pl.pallas_call(
        fourier_kernel,
        out_shape=jax.ShapeDtypeStruct((dests, 32 * steps + 16, LANES), BF16),
        grid=(steps + 1,),
        in_specs=[
            pl.BlockSpec(memory_space=pltpu.SMEM),
            pl.BlockSpec((4, 1, modes, slots), lambda g: (jnp.minimum(g, steps - 1), 0, 0, 0)),
            pl.BlockSpec((modes, slots - 1), lambda g: (0, 0)),
            pl.BlockSpec((144, modes), lambda g: (0, 0)),
            pl.BlockSpec((4, slots, rows), lambda g: (jnp.minimum(g, steps - 1), 0, 0)),
        ],
        out_specs=pl.BlockSpec((dests, 32, LANES), lambda g: (0, g, 0)),
        scratch_shapes=[pltpu.VMEM((rows * 8, LANES), F32), pltpu.VMEM((4 * LANES, rows), F32)],
        name="fourier",
    )(pair_base, ctrl, jnp.transpose(spread), vert, legendre)


def cosine(turns):
    x = turns * math.pi
    y = x * x
    s = -1.0 / 39916800.0
    for c in (1.0 / 362880.0, -1.0 / 5040.0, 1.0 / 120.0, -1.0 / 6.0, 1.0):
        s = s * y + c
    s = s * x
    return 1.0 - 2.0 * (s * s)


def table_kernel(slots, index_ref, owner_ref, main_ref, rest_ref, row_ref, spot_ref):
    cols = index_ref.shape[1]
    depth = main_ref.shape[1]
    waves = depth // 2
    column = jnp.transpose(jnp.broadcast_to(index_ref[...].astype(F32), (LANES, cols)))[:, :1]
    row = jnp.floor((column + 0.5) * (1.0 / NLON))
    longitude = column - row * NLON
    row_ref[...] = jnp.broadcast_to(row, row_ref.shape)
    lane = lax.broadcasted_iota(jnp.int32, (1, depth), 1)

    def fill(ref, source, part, local):
        pair = source * 20 + local // 2
        wave = jnp.where(local % 2 == 0, pair, waves - 1 - pair)
        weight = jnp.where(wave == 0, 1.0, 2.0).astype(F32)
        wave_f = wave.astype(F32)
        shift = part.astype(F32) * (NLON // 4)
        for c in range(0, cols, 64):
            turns = longitude[c : c + 64] * wave_f + shift
            turns = turns - jnp.floor(turns * (1.0 / NLON) + 0.5) * NLON
            ref[c : c + 64, :] = (weight * cosine(turns * (1.0 / NLON))).astype(BF16)

    inner = lane % 80
    fill(main_ref, lane // 80, inner // 40, inner % 40)
    inner = lane % 128
    fill(rest_ref, inner % 32 // 2, inner % 2, inner // 32 * GROUP + lane // 128)

    hits = lax.broadcasted_iota(jnp.int32, (LANES, cols), 0) == owner_ref[...]
    hits_f = jnp.where(hits, 1.0, 0.0).astype(F32)
    before = (
        lax.broadcasted_iota(jnp.int32, (cols, cols), 0)
        < lax.broadcasted_iota(jnp.int32, (cols, cols), 1)
    )
    earlier = dot(hits_f.astype(BF16), jnp.where(before, 1.0, 0.0).astype(BF16))
    first = (lax.broadcasted_iota(jnp.int32, (LANES, cols), 0) * slots).astype(F32)
    spot = jnp.sum(hits_f * (first + earlier), axis=0, keepdims=True).astype(jnp.int32)
    spot_ref[...] = spot


def tables(index, owner, depth, slots):
    cols = index.shape[1]
    return pl.pallas_call(
        functools.partial(table_kernel, slots),
        out_shape=(
            jax.ShapeDtypeStruct((cols, depth), BF16),
            jax.ShapeDtypeStruct((cols, depth), BF16),
            jax.ShapeDtypeStruct((cols, LANES), F32),
            jax.ShapeDtypeStruct((1, cols), jnp.int32),
        ),
        cost_estimate=pl.CostEstimate(
            flops=60 * cols * depth, bytes_accessed=4 << 20, transcendentals=0
        ),
        compiler_params=pltpu.CompilerParams(vmem_limit_bytes=24 << 20),
        name="tables",
    )(index, owner)


def state_kernel(
    main_ref, rest_ref, spot_ref, row_ref, coeff_ref, out_ref, coeff_s, tail_s, take_s, state_s
):
    v = pl.program_id(0)
    cols = main_ref.shape[0]
    depth = main_ref.shape[1]
    sources = coeff_ref.shape[0]
    block = coeff_ref[...].astype(F32).reshape(sources * 2, 22, 8, LANES)
    for r in range(4):
        picked = jnp.stack([block[:, 4 * g + r] for g in range(5)], axis=1)
        coeff_s[:, r * LANES : (r + 1) * LANES] = picked.reshape(depth, LANES).astype(BF16)
    take_s[...] = block[:, 20:].reshape(sources * 2 * 16, LANES)
    lane = lax.broadcasted_iota(jnp.int32, (1, LANES), 1)
    odd = v % 2
    half = pl.ds(pl.multiple_of(v // 2 * LANES, LANES), LANES)
    for u in range(4):
        picked = [take_s[pl.ds(4 * r + u, sources * 2, stride=16), :] for r in range(4)]
        for k in range(GROUP):
            at = (k * 4 + u) * sources * 2
            kept = tail_s[at : at + sources * 2, half]
            for r in range(4):
                moved = pltpu.roll(picked[r], (64 * odd + 16 * r - REST * k + LANES) % LANES, 1)
                kept = jnp.where(lane // 16 == 4 * odd + r, moved, kept)
            tail_s[at : at + sources * 2, half] = kept
    row = row_ref[...]
    products = dot(main_ref[...], coeff_s[...])
    main = products[:, :LANES]
    for r in range(1, 4):
        main = jnp.where(row == r, products[:, r * LANES : (r + 1) * LANES], main)
    state_s[:, pl.ds(pl.multiple_of(v * LANES, LANES), LANES)] = main.astype(BF16)

    @pl.when(v == pl.num_programs(0) - 1)
    def _():
        products = dot(rest_ref[...], tail_s[...].astype(BF16))
        folded = []
        for half in range(2):
            part = products[:, half * LANES : (half + 1) * LANES]
            part = jnp.where((lane // 16 % 4).astype(F32) == row, part, 0.0)
            part = part + pltpu.roll(part, LANES - 32, 1)
            folded.append(part + pltpu.roll(part, LANES - 16, 1))
        tail = jnp.where(lane % 64 < 32, folded[0], pltpu.roll(folded[1], 32, 1))
        state_s[:, 4 * LANES :] = jnp.where(lane % 32 < 9, tail, 0.0).astype(BF16)
        place = lax.broadcasted_iota(jnp.int32, (out_ref.shape[0], cols), 0) == spot_ref[...]
        place = jnp.where(place, 1.0, 0.0).astype(BF16)
        out_ref[...] = dot(place, state_s[...]).astype(BF16)


def column_states(coeff, main_table, rest_table, spot, row, slots):
    sources, rows, _ = coeff.shape
    cols, depth = main_table.shape
    total = slots * LANES
    whole = lambda x: pl.BlockSpec(x.shape, lambda v: (0,) * x.ndim)
    return pl.pallas_call(
        state_kernel,
        out_shape=jax.ShapeDtypeStruct((total, 5 * LANES), BF16),
        grid=(4,),
        in_specs=[
            whole(main_table),
            whole(rest_table),
            whole(spot),
            whole(row),
            pl.BlockSpec((sources, rows // 4, LANES), lambda v: (0, v, 0)),
        ],
        out_specs=pl.BlockSpec((total, 5 * LANES), lambda v: (0, 0)),
        scratch_shapes=[
            pltpu.VMEM((depth, 4 * LANES), BF16),
            pltpu.VMEM((depth, 2 * LANES), F32),
            pltpu.VMEM((sources * 2 * 16, LANES), F32),
            pltpu.VMEM((cols, 5 * LANES), BF16),
        ],
        compiler_params=pltpu.CompilerParams(vmem_limit_bytes=28 << 20),
        name="states",
    )(main_table, rest_table, spot, row, coeff)


def answer_kernel(state_ref, jac_ref, bias_ref, out_ref, jac_s):
    channels = jac_ref.shape[1]
    levels = jac_ref.shape[0] // 4
    rest = levels - LANES

    @pl.when(pl.program_id(0) == 0)
    def _():
        jac = jac_ref[...].astype(F32)
        jac_s[...] = jnp.zeros_like(jac_s)
        for v in range(4):
            at = v * levels
            jac_s[v * LANES : (v + 1) * LANES, :] = jac[at : at + LANES].astype(BF16)
            lo = 4 * LANES + (v % 2 * 2 + v // 2) * SLOT_LANES
            piece = jnp.concatenate(
                [jac[at + LANES : at + levels], jnp.zeros((16 - rest, channels), F32)], axis=0
            )
            jac_s[lo : lo + 16, :] = piece.astype(BF16)

    depart = dot(state_ref[...], jac_s[...]) + bias_ref[...]
    weighted = (depart / jnp.sqrt(1.0 + depart * depart * 0.25)).astype(BF16)
    out_ref[:, :channels] = depart.astype(BF16)
    out_ref[:, 3 * LANES : 3 * LANES + jac_ref.shape[0]] = lax.dot_general(
        weighted, jac_ref[...], (((1,), (1,)), ((), ())), preferred_element_type=F32
    ).astype(BF16)


def answers(states, jac_t, bias):
    total, lanes = states.shape
    width, channels = jac_t.shape
    out_lanes = -(-channels // LANES) * LANES + -(-width // LANES) * LANES
    steps = 2
    return pl.pallas_call(
        answer_kernel,
        out_shape=jax.ShapeDtypeStruct((total, out_lanes), BF16),
        grid=(steps,),
        in_specs=[
            pl.BlockSpec((total // steps, lanes), lambda g: (g, 0)),
            pl.BlockSpec((width, channels), lambda g: (0, 0)),
            pl.BlockSpec((1, channels), lambda g: (0, 0)),
        ],
        out_specs=pl.BlockSpec((total // steps, out_lanes), lambda g: (g, 0)),
        scratch_shapes=[pltpu.VMEM((lanes, channels), BF16)],
        compiler_params=pltpu.CompilerParams(vmem_limit_bytes=20 << 20),
        name="answers",
    )(states, jac_t, bias)


def collect_kernel(spot_ref, back_ref, depart_ref, grad_ref):
    cols = spot_ref.shape[1]
    total = back_ref.shape[0]
    spot = jnp.transpose(jnp.broadcast_to(spot_ref[...].astype(F32), (LANES, cols)))[:, :1]
    place = lax.broadcasted_iota(jnp.int32, (cols, total), 1) == spot.astype(jnp.int32)
    place = jnp.where(place, 1.0, 0.0).astype(BF16)
    channels = depart_ref.shape[0]
    width = grad_ref.shape[0]
    both = jnp.transpose(dot(place, back_ref[...]))
    depart_ref[...] = both[:channels].astype(BF16)
    grad_ref[...] = both[3 * LANES : 3 * LANES + width].astype(BF16)


def collect(spot, back, channels, width):
    cols = spot.shape[1]
    return pl.pallas_call(
        collect_kernel,
        out_shape=(
            jax.ShapeDtypeStruct((channels, cols), BF16),
            jax.ShapeDtypeStruct((width, cols), BF16),
        ),
        compiler_params=pltpu.CompilerParams(vmem_limit_bytes=20 << 20),
        name="collect",
    )(spot, back)


def exchange(x):
    return lax.all_to_all(x, ("wave", "lat"), split_axis=0, concat_axis=0, tiled=True)


def local(control, spread, vertical, legendre, column_index, column_owner, jacobian, channel_bias):
    pairs = control.shape[0]
    wave_count = lax.axis_size("wave")
    device_count = wave_count * lax.axis_size("lat")
    cols = column_index.shape[0]
    slots = max(2, 2 * cols // device_count)
    var = lax.axis_index("lat") // 2
    pair_base = (lax.axis_index("wave") * pairs).astype(jnp.int32).reshape(1)
    blocks = fourier_blocks(control, spread[var], vertical[var], legendre, pair_base, device_count)
    main_table, rest_table, row, spot = tables(
        column_index.reshape(1, cols), column_owner.reshape(1, cols), 4 * pairs * wave_count, slots
    )
    coeff = exchange(blocks).reshape(wave_count, -1, LANES)
    outgoing = column_states(coeff, main_table, rest_table, spot, row, slots)
    lanes = outgoing.shape[1]
    states = exchange(outgoing.reshape(device_count, slots, lanes))
    jac_t = jnp.transpose(jacobian[0])
    reply = answers(states.reshape(device_count * slots, lanes), jac_t, channel_bias)
    back = exchange(reply.reshape(device_count, slots, reply.shape[1]))
    departures, increments = collect(
        spot, back.reshape(device_count * slots, -1), jac_t.shape[1], jac_t.shape[0]
    )
    return (jnp.transpose(departures), jnp.transpose(increments))


def solution(mesh):
    return jax.shard_map(
        local,
        mesh=mesh,
        in_specs=(
            P("wave", None, "lat", None),
            P(),
            P(),
            P("wave", None, None),
            P(("wave", "lat")),
            P(("wave", "lat"), None),
            P(("wave", "lat"), None, None),
            P(("wave", "lat"), None),
        ),
        out_specs=(P(("wave", "lat"), None), P(("wave", "lat"), None)),
        check_vma=False,
    )
```

```python
import functools
import math

import jax
import jax.numpy as jnp
from jax import lax
from jax.experimental import pallas as pl
from jax.experimental.pallas import tpu as pltpu
from jax.sharding import PartitionSpec as P

NLON = 2560
LANES = 128
SLOT_LANES = 32
REST = 12
GROUP = 10
F32 = jnp.float32
BF16 = jnp.bfloat16


def dot(a, b):
    return jnp.dot(a, b, preferred_element_type=F32)


def fourier_kernel(
    base_ref,
    ctrl_ref,
    spread_ref,
    vert_ref,
    leg_ref,
    out_ref,
    main_s,
    rest_s,
    rem_s,
    spread_s,
    second_s,
    first_s,
    scaled_s,
    spec_s,
    vert_s,
):
    slots = ctrl_ref.shape[3]
    waves = slots - 1
    modes = ctrl_ref.shape[2]
    rows = leg_ref.shape[2]
    dests = out_ref.shape[0]
    steps = pl.num_programs(0) - 3
    t = pl.program_id(0)
    lane = lax.broadcasted_iota(jnp.int32, (1, LANES), 1)
    slot = lax.broadcasted_iota(jnp.int32, (1, slots), 1)

    def align(step):
        pair = base_ref[0] + step * 4
        skip = pair // LANES
        shift = pair - skip * LANES
        last = None
        for k in range(6):
            if last is None:
                last = pltpu.roll(
                    spread_s[:, pl.ds(pl.multiple_of(skip * LANES, LANES), LANES)], LANES - shift, 1
                )
            after = spread_s[:, pl.ds(pl.multiple_of((skip + k + 1) * LANES, LANES), LANES)]
            after = pltpu.roll(after, LANES - shift, 1)
            first_s[:, k * LANES : (k + 1) * LANES] = jnp.where(lane < LANES - shift, last, after)
            last = after

    def scale(step, i):
        pair = base_ref[0] + step * 4 + i
        last = first_s[:, :LANES]
        last = pltpu.roll(last, LANES - i, 1) if i else last
        for k in range(5):
            at = slice(k * LANES, (k + 1) * LANES)
            after = first_s[:, (k + 1) * LANES : (k + 2) * LANES]
            after = pltpu.roll(after, LANES - i, 1) if i else after
            factor = jnp.where(lane < LANES - i, last, after) if i else last
            last = after
            if k >= 2:
                factor = jnp.where(lane + k * LANES < waves - pair, factor, second_s[:, at])
            scaled_s[:, at] = (ctrl_ref[i, 0, :, at].astype(F32) * factor).astype(BF16)
        end = ctrl_ref[i, 0, :, waves:].astype(F32) * second_s[:, waves : waves + 1]
        scaled_s[:, waves : waves + 1] = end.astype(BF16)
        spec_s[i] = dot(vert_s[...], scaled_s[:, :slots]).astype(BF16)

    def sums(step, i, early):
        pair = base_ref[0] + step * 4 + i
        spec = spec_s[i]
        lo, hi = (512, slots) if early else (256, 512)
        mixed = spec[:, lo:hi]
        keep = slot[:, lo:hi] < waves - pair
        zero = jnp.zeros_like(mixed)
        both = jnp.concatenate(
            [jnp.where(keep, mixed, zero), jnp.where(keep, zero, mixed)], axis=0
        )
        both = dot(both, leg_ref[i, lo:hi, :])
        half_rows = spec.shape[0]
        first = both[:half_rows] + dot(spec[:, :lo], leg_ref[i, :lo, :])
        second = both[half_rows:]
        if not early:
            second = second + dot(spec[:, hi:], leg_ref[i, hi:, :])
        parts = (first, second)
        for h in range(2):
            j = 2 * i + h
            main_s[pl.ds(j, rows, stride=8), :] = jnp.transpose(parts[h][:LANES])
            rest_s[step, 16 * j : 16 * j + 16, :] = parts[h][LANES:]

    def emit():
        out_ref[...] = main_s[...].reshape(dests, 32, LANES).astype(BF16)

    @pl.when(t == 0)
    def _():
        spread_s[:, waves:] = jnp.zeros((modes, spread_s.shape[1] - waves), F32)
        spread_s[:, :waves] = spread_ref[...]
        second_s[:, :waves] = pltpu.roll(spread_ref[...], 1, 1)
        second_s[:, waves : waves + 1] = spread_ref[:, waves - 1 :]
        vert_s[...] = jnp.zeros_like(vert_s)
        vert_s[:modes, :] = vert_ref[...]
        rem_s[...] = jnp.zeros_like(rem_s)
        align(0)
        for i in range(4):
            scale(0, i)

    for early in (True, False):

        @pl.when((t > 0) & (t <= steps) & ((base_ref[0] + 4 * t <= 128) == early))
        def _():
            emit()
            align(jnp.minimum(t, steps - 1))
            for i in range(4):
                sums(t - 1, i, early)
                scale(jnp.minimum(t, steps - 1), i)

    @pl.when(t == steps + 1)
    def _():
        emit()

    @pl.when(t == steps + 2)
    def _():
        for k in range(8 * steps):
            at = LANES * (k // GROUP) + REST * (k % GROUP)
            lo = 16 * (k % 8)
            rem_s[at : at + REST, :] = rest_s[k // 8, lo : lo + REST, :]
        for u in range(4):
            main_s[pl.ds(u, rows, stride=4), :] = jnp.transpose(rem_s[u * LANES : (u + 1) * LANES])
        out_ref[:, :16, :] = main_s[: 4 * rows, :].reshape(dests, 16, LANES).astype(BF16)


def fourier_blocks(control, spread, vertical, legendre, pair_base, dests):
    pairs, slots, _, modes = control.shape
    rows = legendre.shape[2]
    ctrl = jnp.transpose(control, (0, 2, 3, 1))
    steps = pairs // 4
    return pl.pallas_call(
        fourier_kernel,
        out_shape=jax.ShapeDtypeStruct((dests, 32 * steps + 16, LANES), BF16),
        grid=(steps + 3,),
        in_specs=[
            pl.BlockSpec(memory_space=pltpu.SMEM),
            pl.BlockSpec((4, 1, modes, slots), lambda t: (jnp.minimum(t, steps - 1), 0, 0, 0)),
            pl.BlockSpec((modes, slots - 1), lambda t: (0, 0)),
            pl.BlockSpec((modes, modes), lambda t: (0, 0)),
            pl.BlockSpec((4, slots, rows), lambda t: (jnp.clip(t - 1, 0, steps - 1), 0, 0)),
        ],
        out_specs=pl.BlockSpec((dests, 32, LANES), lambda t: (0, jnp.maximum(t - 2, 0), 0)),
        scratch_shapes=[
            pltpu.VMEM((rows * 8, LANES), F32),
            pltpu.VMEM((steps, LANES, rows), F32),
            pltpu.VMEM((4 * LANES, rows), F32),
            pltpu.VMEM((modes, 9 * LANES), F32),
            pltpu.VMEM((modes, 6 * LANES), F32),
            pltpu.VMEM((modes, 6 * LANES), F32),
            pltpu.VMEM((modes, 6 * LANES), BF16),
            pltpu.VMEM((4, 144, slots), BF16),
            pltpu.VMEM((144, modes), BF16),
        ],
        name="fourier",
    )(pair_base, ctrl, jnp.transpose(spread), vertical, legendre)


def cosine(turns):
    x = turns * math.pi
    y = x * x
    s = -1.0 / 39916800.0
    for c in (1.0 / 362880.0, -1.0 / 5040.0, 1.0 / 120.0, -1.0 / 6.0, 1.0):
        s = s * y + c
    s = s * x
    return 1.0 - 2.0 * (s * s)


def table_kernel(slots, index_ref, owner_ref, main_ref, row_ref, spot_ref):
    cols = index_ref.shape[1]
    depth = main_ref.shape[1]
    waves = depth // 2
    column = jnp.transpose(jnp.broadcast_to(index_ref[...].astype(F32), (LANES, cols)))
    row = jnp.floor((column + 0.5) * (1.0 / NLON))
    row_ref[...] = row
    column = column[:, :1]
    row = row[:, :1]
    longitude = column - row * NLON
    lane = lax.broadcasted_iota(jnp.int32, (1, depth), 1)

    source = lane // 80
    part = lane % 80 // 40
    local = lane % 40
    pair = source * 20 + local // 2
    wave = jnp.where(local % 2 == 0, pair, waves - 1 - pair)
    weight = jnp.where(wave == 0, 1.0, 2.0).astype(F32)
    wave_f = wave.astype(F32)
    shift = part.astype(F32) * (NLON // 4)
    for c in range(0, cols, 64):
        turns = longitude[c : c + 64] * wave_f + shift
        turns = turns - jnp.floor(turns * (1.0 / NLON) + 0.5) * NLON
        main_ref[c : c + 64, :] = (weight * cosine(turns * (1.0 / NLON))).astype(BF16)

    hits = lax.broadcasted_iota(jnp.int32, (LANES, cols), 0) == owner_ref[...]
    hits_f = jnp.where(hits, 1.0, 0.0).astype(F32)
    before = (
        lax.broadcasted_iota(jnp.int32, (cols, cols), 0)
        < lax.broadcasted_iota(jnp.int32, (cols, cols), 1)
    )
    earlier = dot(hits_f.astype(BF16), jnp.where(before, 1.0, 0.0).astype(BF16))
    first = (lax.broadcasted_iota(jnp.int32, (LANES, cols), 0) * slots).astype(F32)
    spot = jnp.sum(hits_f * (first + earlier), axis=0, keepdims=True).astype(jnp.int32)
    spot_ref[...] = spot


def tables(index, owner, depth, slots):
    cols = index.shape[1]
    return pl.pallas_call(
        functools.partial(table_kernel, slots),
        out_shape=(
            jax.ShapeDtypeStruct((cols, depth), BF16),
            jax.ShapeDtypeStruct((cols, LANES), F32),
            jax.ShapeDtypeStruct((1, cols), jnp.int32),
        ),
        cost_estimate=pl.CostEstimate(
            flops=60 * cols * depth, bytes_accessed=4 << 20, transcendentals=0
        ),
        compiler_params=pltpu.CompilerParams(vmem_limit_bytes=24 << 20),
        name="tables",
    )(index, owner)


def state_kernel(
    main_ref, spot_ref, row_ref, coeff_ref, out_ref, coeff_s, tail_s, take_s, state_s
):
    v = pl.program_id(0)
    cols = main_ref.shape[0]
    depth = main_ref.shape[1]
    sources = coeff_ref.shape[0]
    block = coeff_ref[...].astype(F32).reshape(sources * 2, 22, 8, LANES)
    for r in range(4):
        picked = jnp.stack([block[:, 4 * g + r] for g in range(5)], axis=1)
        coeff_s[:, r * LANES : (r + 1) * LANES] = picked.reshape(depth, LANES).astype(BF16)
    take_s[...] = block[:, 20:].reshape(sources * 2 * 16, LANES)
    lane = lax.broadcasted_iota(jnp.int32, (1, LANES), 1)
    odd = v % 2
    for u in range(4):
        picked = [take_s[pl.ds(4 * r + u, sources * 2, stride=16), :] for r in range(4)]
        for k in range(GROUP):
            at = pl.ds(v // 2 * depth + u * GROUP + k, sources * 2, stride=4 * GROUP)
            kept = tail_s[at, :]
            for r in range(4):
                moved = pltpu.roll(picked[r], (64 * odd + 16 * r - REST * k + LANES) % LANES, 1)
                kept = jnp.where(lane // 16 == 4 * odd + r, moved, kept)
            tail_s[at, :] = kept
    row = row_ref[...]
    products = dot(main_ref[...], coeff_s[...])
    main = products[:, :LANES]
    for r in range(1, 4):
        main = jnp.where(row == r, products[:, r * LANES : (r + 1) * LANES], main)
    state_s[:, pl.ds(pl.multiple_of(v * LANES, LANES), LANES)] = main.astype(BF16)

    @pl.when(v == pl.num_programs(0) - 1)
    def _():
        wide = jnp.concatenate([tail_s[:depth], tail_s[depth:]], axis=1)
        products = dot(main_ref[...], wide.astype(BF16))
        folded = []
        for half in range(2):
            part = products[:, half * LANES : (half + 1) * LANES]
            part = jnp.where((lane // 16 % 4).astype(F32) == row, part, 0.0)
            part = part + pltpu.roll(part, LANES - 32, 1)
            folded.append(part + pltpu.roll(part, LANES - 16, 1))
        tail = jnp.where(lane % 64 < 32, folded[0], pltpu.roll(folded[1], 32, 1))
        state_s[:, 4 * LANES :] = jnp.where(lane % 32 < 9, tail, 0.0).astype(BF16)
        place = lax.broadcasted_iota(jnp.int32, (out_ref.shape[0], cols), 0) == spot_ref[...]
        place = jnp.where(place, 1.0, 0.0).astype(BF16)
        out_ref[...] = dot(place, state_s[...]).astype(BF16)


def column_states(coeff, main_table, spot, row, slots):
    sources, rows, _ = coeff.shape
    cols, depth = main_table.shape
    total = slots * LANES
    whole = lambda x: pl.BlockSpec(x.shape, lambda v: (0,) * x.ndim)
    return pl.pallas_call(
        state_kernel,
        out_shape=jax.ShapeDtypeStruct((total, 5 * LANES), BF16),
        grid=(4,),
        in_specs=[
            whole(main_table),
            whole(spot),
            whole(row),
            pl.BlockSpec((sources, rows // 4, LANES), lambda v: (0, v, 0)),
        ],
        out_specs=pl.BlockSpec((total, 5 * LANES), lambda v: (0, 0)),
        scratch_shapes=[
            pltpu.VMEM((depth, 4 * LANES), BF16),
            pltpu.VMEM((2 * depth, LANES), F32),
            pltpu.VMEM((sources * 2 * 16, LANES), F32),
            pltpu.VMEM((cols, 5 * LANES), BF16),
        ],
        compiler_params=pltpu.CompilerParams(vmem_limit_bytes=28 << 20),
        name="states",
    )(main_table, spot, row, coeff)


def answer_kernel(state_ref, jac_ref, bias_ref, out_ref, jac_s):
    channels = jac_ref.shape[1]
    levels = jac_ref.shape[0] // 4
    rest = levels - LANES

    @pl.when(pl.program_id(0) == 0)
    def _():
        jac = jac_ref[...].astype(F32)
        jac_s[...] = jnp.zeros_like(jac_s)
        for v in range(4):
            at = v * levels
            jac_s[v * LANES : (v + 1) * LANES, :] = jac[at : at + LANES].astype(BF16)
            lo = 4 * LANES + (v % 2 * 2 + v // 2) * SLOT_LANES
            piece = jnp.concatenate(
                [jac[at + LANES : at + levels], jnp.zeros((16 - rest, channels), F32)], axis=0
            )
            jac_s[lo : lo + 16, :] = piece.astype(BF16)

    depart = dot(state_ref[...], jac_s[...]) + bias_ref[...]
    weighted = (depart / jnp.sqrt(1.0 + depart * depart * 0.25)).astype(BF16)
    out_ref[:, :channels] = depart.astype(BF16)
    out_ref[:, 3 * LANES : 3 * LANES + jac_ref.shape[0]] = lax.dot_general(
        weighted, jac_ref[...], (((1,), (1,)), ((), ())), preferred_element_type=F32
    ).astype(BF16)


def answers(states, jac_t, bias):
    total, lanes = states.shape
    width, channels = jac_t.shape
    out_lanes = -(-channels // LANES) * LANES + -(-width // LANES) * LANES
    steps = 2
    return pl.pallas_call(
        answer_kernel,
        out_shape=jax.ShapeDtypeStruct((total, out_lanes), BF16),
        grid=(steps,),
        in_specs=[
            pl.BlockSpec((total // steps, lanes), lambda g: (g, 0)),
            pl.BlockSpec((width, channels), lambda g: (0, 0)),
            pl.BlockSpec((1, channels), lambda g: (0, 0)),
        ],
        out_specs=pl.BlockSpec((total // steps, out_lanes), lambda g: (g, 0)),
        scratch_shapes=[pltpu.VMEM((lanes, channels), BF16)],
        compiler_params=pltpu.CompilerParams(vmem_limit_bytes=20 << 20),
        name="answers",
    )(states, jac_t, bias)


def collect_kernel(spot_ref, back_ref, depart_ref, grad_ref):
    cols = spot_ref.shape[1]
    total = back_ref.shape[0]
    spot = jnp.transpose(jnp.broadcast_to(spot_ref[...].astype(F32), (LANES, cols)))[:, :1]
    place = lax.broadcasted_iota(jnp.int32, (cols, total), 1) == spot.astype(jnp.int32)
    place = jnp.where(place, 1.0, 0.0).astype(BF16)
    channels = depart_ref.shape[0]
    width = grad_ref.shape[0]
    both = jnp.transpose(dot(place, back_ref[...]))
    depart_ref[...] = both[:channels].astype(BF16)
    grad_ref[...] = both[3 * LANES : 3 * LANES + width].astype(BF16)


def collect(spot, back, channels, width):
    cols = spot.shape[1]
    return pl.pallas_call(
        collect_kernel,
        out_shape=(
            jax.ShapeDtypeStruct((channels, cols), BF16),
            jax.ShapeDtypeStruct((width, cols), BF16),
        ),
        compiler_params=pltpu.CompilerParams(vmem_limit_bytes=20 << 20),
        name="collect",
    )(spot, back)


def exchange(x):
    return lax.all_to_all(x, ("wave", "lat"), split_axis=0, concat_axis=0, tiled=True)


def local(control, spread, vertical, legendre, column_index, column_owner, jacobian, channel_bias):
    pairs = control.shape[0]
    wave_count = lax.axis_size("wave")
    device_count = wave_count * lax.axis_size("lat")
    cols = column_index.shape[0]
    slots = max(2, 2 * cols // device_count)
    var = lax.axis_index("lat") // 2
    pair_base = (lax.axis_index("wave") * pairs).astype(jnp.int32).reshape(1)
    blocks = fourier_blocks(control, spread[var], vertical[var], legendre, pair_base, device_count)
    index = column_index.reshape(1, cols)
    main_table, row, spot = tables(
        index, column_owner.reshape(1, cols), 4 * pairs * wave_count, slots
    )
    coeff = exchange(blocks).reshape(wave_count, -1, LANES)
    outgoing = column_states(coeff, main_table, spot, row, slots)
    lanes = outgoing.shape[1]
    states = exchange(outgoing.reshape(device_count, slots, lanes))
    jac_t = jnp.transpose(jacobian[0])
    reply = answers(states.reshape(device_count * slots, lanes), jac_t, channel_bias)
    back = exchange(reply.reshape(device_count, slots, reply.shape[1]))
    departures, increments = collect(
        spot, back.reshape(device_count * slots, -1), jac_t.shape[1], jac_t.shape[0]
    )
    return (jnp.transpose(departures), jnp.transpose(increments))


def solution(mesh):
    return jax.shard_map(
        local,
        mesh=mesh,
        in_specs=(
            P("wave", None, "lat", None),
            P(),
            P(),
            P("wave", None, None),
            P(("wave", "lat")),
            P(("wave", "lat"), None),
            P(("wave", "lat"), None, None),
            P(("wave", "lat"), None),
        ),
        out_specs=(P(("wave", "lat"), None), P(("wave", "lat"), None)),
        check_vma=False,
    )
```

```python
import functools
import math

import jax
import jax.numpy as jnp
from jax import lax
from jax.experimental import pallas as pl
from jax.experimental.pallas import tpu as pltpu
from jax.sharding import PartitionSpec as P

NLON = 2560
LANES = 128
SLOT_LANES = 32
REST = 12
GROUP = 10
F32 = jnp.float32
BF16 = jnp.bfloat16


def dot(a, b):
    return jnp.dot(a, b, preferred_element_type=F32)


def fourier_kernel(
    base_ref,
    ctrl_ref,
    spread_ref,
    vert_ref,
    leg_ref,
    out_ref,
    main_s,
    rest_s,
    rem_s,
    spread_s,
    second_s,
    first_s,
    scaled_s,
    spec_s,
    vert_s,
):
    slots = ctrl_ref.shape[3]
    waves = slots - 1
    modes = ctrl_ref.shape[2]
    rows = leg_ref.shape[2]
    dests = out_ref.shape[0]
    steps = pl.num_programs(0) - 3
    t = pl.program_id(0)
    lane = lax.broadcasted_iota(jnp.int32, (1, LANES), 1)
    slot = lax.broadcasted_iota(jnp.int32, (1, slots), 1)

    def align(step):
        pair = base_ref[0] + step * 4
        skip = pair // LANES
        shift = pair - skip * LANES
        last = None
        for k in range(6):
            if last is None:
                last = pltpu.roll(
                    spread_s[:, pl.ds(pl.multiple_of(skip * LANES, LANES), LANES)], LANES - shift, 1
                )
            after = spread_s[:, pl.ds(pl.multiple_of((skip + k + 1) * LANES, LANES), LANES)]
            after = pltpu.roll(after, LANES - shift, 1)
            first_s[:, k * LANES : (k + 1) * LANES] = jnp.where(lane < LANES - shift, last, after)
            last = after

    def scale(step, i):
        pair = base_ref[0] + step * 4 + i
        last = first_s[:, :LANES]
        last = pltpu.roll(last, LANES - i, 1) if i else last
        for k in range(5):
            at = slice(k * LANES, (k + 1) * LANES)
            after = first_s[:, (k + 1) * LANES : (k + 2) * LANES]
            after = pltpu.roll(after, LANES - i, 1) if i else after
            factor = jnp.where(lane < LANES - i, last, after) if i else last
            last = after
            if k >= 2:
                factor = jnp.where(lane + k * LANES < waves - pair, factor, second_s[:, at])
            scaled_s[:, at] = (ctrl_ref[i, 0, :, at].astype(F32) * factor).astype(BF16)
        end = ctrl_ref[i, 0, :, waves:].astype(F32) * second_s[:, waves : waves + 1]
        scaled_s[:, waves : waves + 1] = end.astype(BF16)
        spec_s[i] = dot(vert_s[...], scaled_s[:, :slots]).astype(BF16)

    def sums(step, i, early):
        pair = base_ref[0] + step * 4 + i
        spec = spec_s[i]
        lo, hi = (512, slots) if early else (256, 512)
        mixed = spec[:, lo:hi]
        keep = slot[:, lo:hi] < waves - pair
        zero = jnp.zeros_like(mixed)
        both = jnp.concatenate(
            [jnp.where(keep, mixed, zero), jnp.where(keep, zero, mixed)], axis=0
        )
        both = dot(both, leg_ref[i, lo:hi, :])
        half_rows = spec.shape[0]
        first = both[:half_rows] + dot(spec[:, :lo], leg_ref[i, :lo, :])
        second = both[half_rows:]
        if not early:
            second = second + dot(spec[:, hi:], leg_ref[i, hi:, :])
        parts = (first, second)
        for h in range(2):
            j = 2 * i + h
            main_s[pl.ds(j, rows, stride=8), :] = jnp.transpose(parts[h][:LANES])
            rest_s[step, 16 * j : 16 * j + 16, :] = parts[h][LANES:]

    def emit():
        out_ref[...] = main_s[...].reshape(dests, 32, LANES).astype(BF16)

    @pl.when(t == 0)
    def _():
        spread_s[:, waves:] = jnp.zeros((modes, spread_s.shape[1] - waves), F32)
        spread_s[:, :waves] = spread_ref[...]
        second_s[:, :waves] = pltpu.roll(spread_ref[...], 1, 1)
        second_s[:, waves : waves + 1] = spread_ref[:, waves - 1 :]
        vert_s[...] = jnp.zeros_like(vert_s)
        vert_s[:modes, :] = vert_ref[...]
        rem_s[...] = jnp.zeros_like(rem_s)
        align(0)
        for i in range(4):
            scale(0, i)

    for early in (True, False):

        @pl.when((t > 0) & (t <= steps) & ((base_ref[0] + 4 * t <= 128) == early))
        def _():
            emit()
            align(jnp.minimum(t, steps - 1))
            for i in range(4):
                sums(t - 1, i, early)
                scale(jnp.minimum(t, steps - 1), i)

    @pl.when(t == steps + 1)
    def _():
        emit()

    @pl.when(t == steps + 2)
    def _():
        for k in range(8 * steps):
            at = LANES * (k // GROUP) + REST * (k % GROUP)
            lo = 16 * (k % 8)
            rem_s[at : at + REST, :] = rest_s[k // 8, lo : lo + REST, :]
        for u in range(4):
            main_s[pl.ds(u, rows, stride=4), :] = jnp.transpose(rem_s[u * LANES : (u + 1) * LANES])
        out_ref[:, :16, :] = main_s[: 4 * rows, :].reshape(dests, 16, LANES).astype(BF16)


def fourier_blocks(control, spread, vertical, legendre, pair_base, dests):
    pairs, slots, _, modes = control.shape
    rows = legendre.shape[2]
    ctrl = jnp.transpose(control, (0, 2, 3, 1))
    steps = pairs // 4
    return pl.pallas_call(
        fourier_kernel,
        out_shape=jax.ShapeDtypeStruct((dests, 32 * steps + 16, LANES), BF16),
        grid=(steps + 3,),
        in_specs=[
            pl.BlockSpec(memory_space=pltpu.SMEM),
            pl.BlockSpec((4, 1, modes, slots), lambda t: (jnp.minimum(t, steps - 1), 0, 0, 0)),
            pl.BlockSpec((modes, slots - 1), lambda t: (0, 0)),
            pl.BlockSpec((modes, modes), lambda t: (0, 0)),
            pl.BlockSpec((4, slots, rows), lambda t: (jnp.clip(t - 1, 0, steps - 1), 0, 0)),
        ],
        out_specs=pl.BlockSpec((dests, 32, LANES), lambda t: (0, jnp.maximum(t - 2, 0), 0)),
        scratch_shapes=[
            pltpu.VMEM((rows * 8, LANES), F32),
            pltpu.VMEM((steps, LANES, rows), F32),
            pltpu.VMEM((4 * LANES, rows), F32),
            pltpu.VMEM((modes, 9 * LANES), F32),
            pltpu.VMEM((modes, 6 * LANES), F32),
            pltpu.VMEM((modes, 6 * LANES), F32),
            pltpu.VMEM((modes, 6 * LANES), BF16),
            pltpu.VMEM((4, 144, slots), BF16),
            pltpu.VMEM((144, modes), BF16),
        ],
        name="fourier",
    )(pair_base, ctrl, jnp.transpose(spread), vertical, legendre)


def cosine(turns):
    x = turns * math.pi
    y = x * x
    s = -1.0 / 39916800.0
    for c in (1.0 / 362880.0, -1.0 / 5040.0, 1.0 / 120.0, -1.0 / 6.0, 1.0):
        s = s * y + c
    s = s * x
    return 1.0 - 2.0 * (s * s)


def table_kernel(slots, index_ref, owner_ref, main_ref, row_ref, spot_ref):
    cols = index_ref.shape[1]
    depth = main_ref.shape[1]
    waves = depth // 2
    column = jnp.transpose(jnp.broadcast_to(index_ref[...].astype(F32), (LANES, cols)))
    row = jnp.floor((column + 0.5) * (1.0 / NLON))
    row_ref[...] = row
    column = column[:, :1]
    row = row[:, :1]
    longitude = column - row * NLON
    lane = lax.broadcasted_iota(jnp.int32, (1, depth), 1)

    source = lane // 80
    part = lane % 80 // 40
    local = lane % 40
    pair = source * 20 + local // 2
    wave = jnp.where(local % 2 == 0, pair, waves - 1 - pair)
    weight = jnp.where(wave == 0, 1.0, 2.0).astype(F32)
    wave_f = wave.astype(F32)
    shift = part.astype(F32) * (NLON // 4)
    for c in range(0, cols, 64):
        turns = longitude[c : c + 64] * wave_f + shift
        turns = turns - jnp.floor(turns * (1.0 / NLON) + 0.5) * NLON
        main_ref[c : c + 64, :] = (weight * cosine(turns * (1.0 / NLON))).astype(BF16)

    hits = lax.broadcasted_iota(jnp.int32, (LANES, cols), 0) == owner_ref[...]
    hits_f = jnp.where(hits, 1.0, 0.0).astype(F32)
    before = (
        lax.broadcasted_iota(jnp.int32, (cols, cols), 0)
        < lax.broadcasted_iota(jnp.int32, (cols, cols), 1)
    )
    earlier = dot(hits_f.astype(BF16), jnp.where(before, 1.0, 0.0).astype(BF16))
    first = (lax.broadcasted_iota(jnp.int32, (LANES, cols), 0) * slots).astype(F32)
    spot = jnp.sum(hits_f * (first + earlier), axis=0, keepdims=True).astype(jnp.int32)
    spot_ref[...] = spot


def tables(index, owner, depth, slots):
    cols = index.shape[1]
    return pl.pallas_call(
        functools.partial(table_kernel, slots),
        out_shape=(
            jax.ShapeDtypeStruct((cols, depth), BF16),
            jax.ShapeDtypeStruct((cols, LANES), F32),
            jax.ShapeDtypeStruct((1, cols), jnp.int32),
        ),
        cost_estimate=pl.CostEstimate(
            flops=60 * cols * depth, bytes_accessed=4 << 20, transcendentals=0
        ),
        compiler_params=pltpu.CompilerParams(vmem_limit_bytes=24 << 20),
        name="tables",
    )(index, owner)


def state_kernel(
    main_ref, spot_ref, row_ref, coeff_ref, out_ref, coeff_s, tail_s, take_s, state_s
):
    v = pl.program_id(0)
    cols = main_ref.shape[0]
    depth = main_ref.shape[1]
    sources = coeff_ref.shape[0]
    block = coeff_ref[...].astype(F32).reshape(sources * 2, 22, 8, LANES)
    for r in range(4):
        picked = jnp.stack([block[:, 4 * g + r] for g in range(5)], axis=1)
        coeff_s[:, r * LANES : (r + 1) * LANES] = picked.reshape(depth, LANES).astype(BF16)
    take_s[...] = block[:, 20:].reshape(sources * 2 * 16, LANES)
    lane = lax.broadcasted_iota(jnp.int32, (1, LANES), 1)
    odd = v % 2
    for u in range(4):
        picked = [take_s[pl.ds(4 * r + u, sources * 2, stride=16), :] for r in range(4)]
        for k in range(GROUP):
            at = pl.ds(v // 2 * depth + u * GROUP + k, sources * 2, stride=4 * GROUP)
            kept = tail_s[at, :]
            for r in range(4):
                moved = pltpu.roll(picked[r], (64 * odd + 16 * r - REST * k + LANES) % LANES, 1)
                kept = jnp.where(lane // 16 == 4 * odd + r, moved, kept)
            tail_s[at, :] = kept
    row = row_ref[...]
    products = dot(main_ref[...], coeff_s[...])
    main = products[:, :LANES]
    for r in range(1, 4):
        main = jnp.where(row == r, products[:, r * LANES : (r + 1) * LANES], main)
    state_s[:, pl.ds(pl.multiple_of(v * LANES, LANES), LANES)] = main.astype(BF16)

    @pl.when(v == pl.num_programs(0) - 1)
    def _():
        wide = jnp.concatenate([tail_s[:depth], tail_s[depth:]], axis=1)
        products = dot(main_ref[...], wide.astype(BF16))
        folded = []
        for half in range(2):
            part = products[:, half * LANES : (half + 1) * LANES]
            part = jnp.where((lane // 16 % 4).astype(F32) == row, part, 0.0)
            part = part + pltpu.roll(part, LANES - 32, 1)
            folded.append(part + pltpu.roll(part, LANES - 16, 1))
        tail = jnp.where(lane % 64 < 32, folded[0], pltpu.roll(folded[1], 32, 1))
        state_s[:, 4 * LANES :] = jnp.where(lane % 32 < 9, tail, 0.0).astype(BF16)
        place = lax.broadcasted_iota(jnp.int32, (out_ref.shape[0], cols), 0) == spot_ref[...]
        place = jnp.where(place, 1.0, 0.0).astype(BF16)
        out_ref[...] = dot(place, state_s[...]).astype(BF16)


def column_states(coeff, main_table, spot, row, slots):
    sources, rows, _ = coeff.shape
    cols, depth = main_table.shape
    total = slots * LANES
    whole = lambda x: pl.BlockSpec(x.shape, lambda v: (0,) * x.ndim)
    return pl.pallas_call(
        state_kernel,
        out_shape=jax.ShapeDtypeStruct((total, 5 * LANES), BF16),
        grid=(4,),
        in_specs=[
            whole(main_table),
            whole(spot),
            whole(row),
            pl.BlockSpec((sources, rows // 4, LANES), lambda v: (0, v, 0)),
        ],
        out_specs=pl.BlockSpec((total, 5 * LANES), lambda v: (0, 0)),
        scratch_shapes=[
            pltpu.VMEM((depth, 4 * LANES), BF16),
            pltpu.VMEM((2 * depth, LANES), F32),
            pltpu.VMEM((sources * 2 * 16, LANES), F32),
            pltpu.VMEM((cols, 5 * LANES), BF16),
        ],
        compiler_params=pltpu.CompilerParams(vmem_limit_bytes=28 << 20),
        name="states",
    )(main_table, spot, row, coeff)


def jacobian_kernel(jac_ref, bias_ref, out_ref):
    channels = jac_ref.shape[1]
    levels = jac_ref.shape[0] // 4
    jac = jac_ref[...].astype(F32)
    out_ref[...] = jnp.zeros_like(out_ref)
    for v in range(4):
        at = v * levels
        out_ref[v * LANES : (v + 1) * LANES, :] = jac[at : at + LANES].astype(BF16)
        lo = 4 * LANES + (v % 2 * 2 + v // 2) * SLOT_LANES
        pad = jnp.zeros((16 - (levels - LANES), channels), F32)
        piece = jnp.concatenate([jac[at + LANES : at + levels], pad], axis=0)
        out_ref[lo : lo + 16, :] = piece.astype(BF16)
    parts = []
    left = bias_ref[...]
    for _ in range(3):
        parts.append(left.astype(BF16).astype(F32))
        left = left - parts[-1]
    parts.append(jnp.zeros((13, channels), F32))
    out_ref[5 * LANES :, :] = jnp.concatenate(parts, axis=0).astype(BF16)


def owner_table(jac_t, bias):
    return pl.pallas_call(
        jacobian_kernel,
        out_shape=jax.ShapeDtypeStruct((5 * LANES + 16, jac_t.shape[1]), BF16),
        compiler_params=pltpu.CompilerParams(vmem_limit_bytes=16 << 20),
        name="jacobians",
    )(jac_t, bias)


def answer_kernel(place_ref, state_ref, own_ref, other_ref, out_ref):
    width = 5 * LANES
    sources = state_ref.shape[0]
    channels = own_ref.shape[2]
    rows = sources * 8
    first = place_ref[1] == 0
    states = state_ref[...].astype(F32)
    low, high = states[:, :8].reshape(rows, width), states[:, 8:].reshape(rows, width)

    def answer(state, jac_ref):
        bias = jnp.sum(jac_ref[0, width:, :].astype(F32), axis=0, keepdims=True)
        depart = dot(state.astype(BF16), jac_ref[0, :width, :]) + bias
        weighted = (depart / jnp.sqrt(1.0 + depart * depart * 0.25)).astype(BF16)
        grad = lax.dot_general(
            weighted, jac_ref[0, :width, :], (((1,), (1,)), ((), ())), preferred_element_type=F32
        )
        return depart, grad

    own = answer(jnp.where(first, low, high), own_ref)
    other = answer(jnp.where(first, high, low), other_ref)
    for part, at in ((0, 0), (1, 3 * LANES)):
        size = own[part].shape[1]
        low = jnp.where(first, own[part], other[part]).reshape(sources, 8, size)
        high = jnp.where(first, other[part], own[part]).reshape(sources, 8, size)
        both = jnp.concatenate([low, high], axis=1)
        out_ref[:, :, at : at + size] = both.astype(BF16)


def answers(states, place, own, other):
    sources, rows, width = states.shape
    chips, depth, channels = own.shape
    pick = lambda g, place: ((place[0] - g + chips) % chips, 0, 0)
    return pl.pallas_call(
        answer_kernel,
        out_shape=jax.ShapeDtypeStruct((sources, rows, 8 * LANES), BF16),
        grid_spec=pltpu.PrefetchScalarGridSpec(
            num_scalar_prefetch=1,
            grid=(chips,),
            in_specs=[
                pl.BlockSpec((sources, rows // chips, width), lambda g, place: (0, g, 0)),
                pl.BlockSpec((1, depth, channels), pick),
                pl.BlockSpec((1, depth, channels), pick),
            ],
            out_specs=pl.BlockSpec((sources, rows // chips, 8 * LANES), lambda g, place: (0, g, 0)),
        ),
        compiler_params=pltpu.CompilerParams(vmem_limit_bytes=20 << 20),
        name="answers",
    )(place, states, own, other)


def collect_kernel(spot_ref, back_ref, depart_ref, grad_ref):
    cols = spot_ref.shape[1]
    total = back_ref.shape[0]
    spot = jnp.transpose(jnp.broadcast_to(spot_ref[...].astype(F32), (LANES, cols)))[:, :1]
    place = lax.broadcasted_iota(jnp.int32, (cols, total), 1) == spot.astype(jnp.int32)
    place = jnp.where(place, 1.0, 0.0).astype(BF16)
    channels = depart_ref.shape[0]
    width = grad_ref.shape[0]
    both = jnp.transpose(dot(place, back_ref[...]))
    depart_ref[...] = both[:channels].astype(BF16)
    levels = width // 4
    parts = []
    for v in range(4):
        lo = 7 * LANES + (v % 2 * 2 + v // 2) * SLOT_LANES
        parts.append(both[(3 + v) * LANES : (4 + v) * LANES])
        parts.append(both[lo : lo + levels - LANES])
    grad_ref[...] = jnp.concatenate(parts, axis=0).astype(BF16)


def collect(spot, back, channels, width):
    cols = spot.shape[1]
    return pl.pallas_call(
        collect_kernel,
        out_shape=(
            jax.ShapeDtypeStruct((channels, cols), BF16),
            jax.ShapeDtypeStruct((width, cols), BF16),
        ),
        compiler_params=pltpu.CompilerParams(vmem_limit_bytes=20 << 20),
        name="collect",
    )(spot, back)


def exchange(x, axes):
    return lax.all_to_all(x, axes, split_axis=0, concat_axis=0, tiled=True)


def chip_tables(table, lat_count):
    ring = lambda step: [(i, (i + 2 * step) % lat_count) for i in range(lat_count)]
    parts = [table] + [lax.ppermute(table, "lat", ring(step)) for step in range(1, lat_count // 2)]
    own = pltpu.with_memory_space_constraint(jnp.stack(parts), pltpu.HBM)
    return own, lax.ppermute(own, "lat", [(i, i ^ 1) for i in range(lat_count)])


def local(control, spread, vertical, legendre, column_index, column_owner, jacobian, channel_bias):
    pairs = control.shape[0]
    wave_count = lax.axis_size("wave")
    device_count = wave_count * lax.axis_size("lat")
    cols = column_index.shape[0]
    slots = max(2, 2 * cols // device_count)
    var = lax.axis_index("lat") // 2
    pair_base = (lax.axis_index("wave") * pairs).astype(jnp.int32).reshape(1)
    blocks = fourier_blocks(control, spread[var], vertical[var], legendre, pair_base, device_count)
    index = column_index.reshape(1, cols)
    main_table, row, spot = tables(
        index, column_owner.reshape(1, cols), 4 * pairs * wave_count, slots
    )
    lat = lax.axis_index("lat").astype(jnp.int32)
    jac_t = jnp.transpose(jacobian[0])
    own, other = chip_tables(owner_table(jac_t, channel_bias), lax.axis_size("lat"))
    coeff = exchange(blocks, ("wave", "lat")).reshape(wave_count, -1, LANES)
    outgoing = column_states(coeff, main_table, spot, row, slots)
    lanes = outgoing.shape[1]
    states = exchange(outgoing.reshape(wave_count, -1, lanes), "wave")
    reply = answers(states, jnp.stack([lat // 2, lat % 2]), own, other)
    back = exchange(reply, "wave")
    departures, increments = collect(
        spot, back.reshape(device_count * slots, -1), jac_t.shape[1], jac_t.shape[0]
    )
    return (jnp.transpose(departures), jnp.transpose(increments))


def solution(mesh):
    return jax.shard_map(
        local,
        mesh=mesh,
        in_specs=(
            P("wave", None, "lat", None),
            P(),
            P(),
            P("wave", None, None),
            P(("wave", "lat")),
            P(("wave", "lat"), None),
            P(("wave", "lat"), None, None),
            P(("wave", "lat"), None),
        ),
        out_specs=(P(("wave", "lat"), None), P(("wave", "lat"), None)),
        check_vma=False,
    )
```

```python
import functools
import math

import jax
import jax.numpy as jnp
from jax import lax
from jax.experimental import pallas as pl
from jax.experimental.pallas import tpu as pltpu
from jax.sharding import Mesh, PartitionSpec as P

NLON = 2560
LANES = 128
SLOT_LANES = 32
REST = 12
GROUP = 10
F32 = jnp.float32
BF16 = jnp.bfloat16


def dot(a, b):
    return jnp.dot(a, b, preferred_element_type=F32)


def fourier_kernel(
    base_ref,
    ctrl_ref,
    spread_ref,
    vert_ref,
    leg_ref,
    out_ref,
    main_s,
    rest_s,
    rem_s,
    spread_s,
    second_s,
    first_s,
    scaled_s,
    spec_s,
    vert_s,
):
    slots = ctrl_ref.shape[3]
    waves = slots - 1
    modes = ctrl_ref.shape[2]
    rows = leg_ref.shape[2]
    dests = out_ref.shape[0]
    steps = pl.num_programs(0) - 3
    t = pl.program_id(0)
    lane = lax.broadcasted_iota(jnp.int32, (1, LANES), 1)
    slot = lax.broadcasted_iota(jnp.int32, (1, slots), 1)

    def align(step):
        pair = base_ref[0] + step * 4
        skip = pair // LANES
        shift = pair - skip * LANES
        last = None
        for k in range(6):
            if last is None:
                last = pltpu.roll(
                    spread_s[:, pl.ds(pl.multiple_of(skip * LANES, LANES), LANES)], LANES - shift, 1
                )
            after = spread_s[:, pl.ds(pl.multiple_of((skip + k + 1) * LANES, LANES), LANES)]
            after = pltpu.roll(after, LANES - shift, 1)
            first_s[:, k * LANES : (k + 1) * LANES] = jnp.where(lane < LANES - shift, last, after)
            last = after

    def scale(step, i):
        pair = base_ref[0] + step * 4 + i
        last = first_s[:, :LANES]
        last = pltpu.roll(last, LANES - i, 1) if i else last
        for k in range(5):
            at = slice(k * LANES, (k + 1) * LANES)
            after = first_s[:, (k + 1) * LANES : (k + 2) * LANES]
            after = pltpu.roll(after, LANES - i, 1) if i else after
            factor = jnp.where(lane < LANES - i, last, after) if i else last
            last = after
            if k >= 2:
                factor = jnp.where(lane + k * LANES < waves - pair, factor, second_s[:, at])
            scaled_s[:, at] = (ctrl_ref[i, 0, :, at].astype(F32) * factor).astype(BF16)
        end = ctrl_ref[i, 0, :, waves:].astype(F32) * second_s[:, waves : waves + 1]
        scaled_s[:, waves : waves + 1] = end.astype(BF16)
        spec_s[i] = dot(vert_s[...], scaled_s[:, :slots]).astype(BF16)

    def sums(step, i, early):
        pair = base_ref[0] + step * 4 + i
        spec = spec_s[i]
        lo, hi = (512, slots) if early else (256, 512)
        mixed = spec[:, lo:hi]
        keep = slot[:, lo:hi] < waves - pair
        zero = jnp.zeros_like(mixed)
        both = jnp.concatenate(
            [jnp.where(keep, mixed, zero), jnp.where(keep, zero, mixed)], axis=0
        )
        both = dot(both, leg_ref[i, lo:hi, :])
        half_rows = spec.shape[0]
        first = both[:half_rows] + dot(spec[:, :lo], leg_ref[i, :lo, :])
        second = both[half_rows:]
        if not early:
            second = second + dot(spec[:, hi:], leg_ref[i, hi:, :])
        parts = (first, second)
        for h in range(2):
            j = 2 * i + h
            main_s[pl.ds(j, rows, stride=8), :] = jnp.transpose(parts[h][:LANES])
            rest_s[step, 16 * j : 16 * j + 16, :] = parts[h][LANES:]

    def emit():
        out_ref[...] = main_s[...].reshape(dests, 32, LANES).astype(BF16)

    @pl.when(t == 0)
    def _():
        spread_s[:, waves:] = jnp.zeros((modes, spread_s.shape[1] - waves), F32)
        spread_s[:, :waves] = spread_ref[...]
        second_s[:, :waves] = pltpu.roll(spread_ref[...], 1, 1)
        second_s[:, waves : waves + 1] = spread_ref[:, waves - 1 :]
        vert_s[...] = jnp.zeros_like(vert_s)
        vert_s[:modes, :] = vert_ref[...]
        rem_s[...] = jnp.zeros_like(rem_s)
        align(0)
        for i in range(4):
            scale(0, i)

    for early in (True, False):

        @pl.when((t > 0) & (t <= steps) & ((base_ref[0] + 4 * t <= 128) == early))
        def _():
            emit()
            align(jnp.minimum(t, steps - 1))
            for i in range(4):
                sums(t - 1, i, early)
                scale(jnp.minimum(t, steps - 1), i)

    @pl.when(t == steps + 1)
    def _():
        emit()

    @pl.when(t == steps + 2)
    def _():
        for k in range(8 * steps):
            at = LANES * (k // GROUP) + REST * (k % GROUP)
            lo = 16 * (k % 8)
            rem_s[at : at + REST, :] = rest_s[k // 8, lo : lo + REST, :]
        for u in range(4):
            main_s[pl.ds(u, rows, stride=4), :] = jnp.transpose(rem_s[u * LANES : (u + 1) * LANES])
        out_ref[:, :16, :] = main_s[: 4 * rows, :].reshape(dests, 16, LANES).astype(BF16)


def fourier_blocks(control, spread, vertical, legendre, pair_base, dests):
    pairs, slots, _, modes = control.shape
    rows = legendre.shape[2]
    ctrl = jnp.transpose(control, (0, 2, 3, 1))
    steps = pairs // 4
    return pl.pallas_call(
        fourier_kernel,
        out_shape=jax.ShapeDtypeStruct((dests, 32 * steps + 16, LANES), BF16),
        grid=(steps + 3,),
        in_specs=[
            pl.BlockSpec(memory_space=pltpu.SMEM),
            pl.BlockSpec((4, 1, modes, slots), lambda t: (jnp.minimum(t, steps - 1), 0, 0, 0)),
            pl.BlockSpec((modes, slots - 1), lambda t: (0, 0)),
            pl.BlockSpec((modes, modes), lambda t: (0, 0)),
            pl.BlockSpec((4, slots, rows), lambda t: (jnp.clip(t - 1, 0, steps - 1), 0, 0)),
        ],
        out_specs=pl.BlockSpec((dests, 32, LANES), lambda t: (0, jnp.maximum(t - 2, 0), 0)),
        scratch_shapes=[
            pltpu.VMEM((rows * 8, LANES), F32),
            pltpu.VMEM((steps, LANES, rows), F32),
            pltpu.VMEM((4 * LANES, rows), F32),
            pltpu.VMEM((modes, 9 * LANES), F32),
            pltpu.VMEM((modes, 6 * LANES), F32),
            pltpu.VMEM((modes, 6 * LANES), F32),
            pltpu.VMEM((modes, 6 * LANES), BF16),
            pltpu.VMEM((4, 144, slots), BF16),
            pltpu.VMEM((144, modes), BF16),
        ],
        name="fourier",
    )(pair_base, ctrl, jnp.transpose(spread), vertical, legendre)


def cosine(turns):
    x = turns * math.pi
    y = x * x
    s = -1.0 / 39916800.0
    for c in (1.0 / 362880.0, -1.0 / 5040.0, 1.0 / 120.0, -1.0 / 6.0, 1.0):
        s = s * y + c
    s = s * x
    return 1.0 - 2.0 * (s * s)


def table_kernel(slots, index_ref, owner_ref, main_ref, row_ref, spot_ref):
    cols = index_ref.shape[1]
    depth = main_ref.shape[1]
    waves = depth // 2
    column = jnp.transpose(jnp.broadcast_to(index_ref[...].astype(F32), (LANES, cols)))
    row = jnp.floor((column + 0.5) * (1.0 / NLON))
    row_ref[...] = row
    column = column[:, :1]
    row = row[:, :1]
    longitude = column - row * NLON
    lane = lax.broadcasted_iota(jnp.int32, (1, depth), 1)

    source = lane // 80
    part = lane % 80 // 40
    local = lane % 40
    pair = source * 20 + local // 2
    wave = jnp.where(local % 2 == 0, pair, waves - 1 - pair)
    weight = jnp.where(wave == 0, 1.0, 2.0).astype(F32)
    wave_f = wave.astype(F32)
    shift = part.astype(F32) * (NLON // 4)
    for c in range(0, cols, 64):
        turns = longitude[c : c + 64] * wave_f + shift
        turns = turns - jnp.floor(turns * (1.0 / NLON) + 0.5) * NLON
        main_ref[c : c + 64, :] = (weight * cosine(turns * (1.0 / NLON))).astype(BF16)

    hits = lax.broadcasted_iota(jnp.int32, (LANES, cols), 0) == owner_ref[...]
    hits_f = jnp.where(hits, 1.0, 0.0).astype(F32)
    before = (
        lax.broadcasted_iota(jnp.int32, (cols, cols), 0)
        < lax.broadcasted_iota(jnp.int32, (cols, cols), 1)
    )
    earlier = dot(hits_f.astype(BF16), jnp.where(before, 1.0, 0.0).astype(BF16))
    first = (lax.broadcasted_iota(jnp.int32, (LANES, cols), 0) * slots).astype(F32)
    spot = jnp.sum(hits_f * (first + earlier), axis=0, keepdims=True).astype(jnp.int32)
    spot_ref[...] = spot


def tables(index, owner, depth, slots):
    cols = index.shape[1]
    return pl.pallas_call(
        functools.partial(table_kernel, slots),
        out_shape=(
            jax.ShapeDtypeStruct((cols, depth), BF16),
            jax.ShapeDtypeStruct((cols, LANES), F32),
            jax.ShapeDtypeStruct((1, cols), jnp.int32),
        ),
        cost_estimate=pl.CostEstimate(
            flops=60 * cols * depth, bytes_accessed=4 << 20, transcendentals=0
        ),
        compiler_params=pltpu.CompilerParams(vmem_limit_bytes=24 << 20),
        name="tables",
    )(index, owner)


def state_kernel(
    main_ref, spot_ref, row_ref, coeff_ref, out_ref, coeff_s, tail_s, take_s, state_s
):
    v = pl.program_id(0)
    cols = main_ref.shape[0]
    depth = main_ref.shape[1]
    sources = coeff_ref.shape[0]
    block = coeff_ref[...].astype(F32).reshape(sources * 2, 22, 8, LANES)
    for r in range(4):
        picked = jnp.stack([block[:, 4 * g + r] for g in range(5)], axis=1)
        coeff_s[:, r * LANES : (r + 1) * LANES] = picked.reshape(depth, LANES).astype(BF16)
    take_s[...] = block[:, 20:].reshape(sources * 2 * 16, LANES)
    lane = lax.broadcasted_iota(jnp.int32, (1, LANES), 1)
    odd = v % 2
    for u in range(4):
        picked = [take_s[pl.ds(4 * r + u, sources * 2, stride=16), :] for r in range(4)]
        for k in range(GROUP):
            at = pl.ds(v // 2 * depth + u * GROUP + k, sources * 2, stride=4 * GROUP)
            kept = tail_s[at, :]
            for r in range(4):
                moved = pltpu.roll(picked[r], (64 * odd + 16 * r - REST * k + LANES) % LANES, 1)
                kept = jnp.where(lane // 16 == 4 * odd + r, moved, kept)
            tail_s[at, :] = kept
    row = row_ref[...]
    products = dot(main_ref[...], coeff_s[...])
    main = products[:, :LANES]
    for r in range(1, 4):
        main = jnp.where(row == r, products[:, r * LANES : (r + 1) * LANES], main)
    state_s[:, pl.ds(pl.multiple_of(v * LANES, LANES), LANES)] = main.astype(BF16)

    @pl.when(v == pl.num_programs(0) - 1)
    def _():
        wide = jnp.concatenate([tail_s[:depth], tail_s[depth:]], axis=1)
        products = dot(main_ref[...], wide.astype(BF16))
        folded = []
        for half in range(2):
            part = products[:, half * LANES : (half + 1) * LANES]
            part = jnp.where((lane // 16 % 4).astype(F32) == row, part, 0.0)
            part = part + pltpu.roll(part, LANES - 32, 1)
            folded.append(part + pltpu.roll(part, LANES - 16, 1))
        tail = jnp.where(lane % 64 < 32, folded[0], pltpu.roll(folded[1], 32, 1))
        state_s[:, 4 * LANES :] = jnp.where(lane % 32 < 9, tail, 0.0).astype(BF16)
        place = lax.broadcasted_iota(jnp.int32, (out_ref.shape[0], cols), 0) == spot_ref[...]
        place = jnp.where(place, 1.0, 0.0).astype(BF16)
        out_ref[...] = dot(place, state_s[...]).astype(BF16)


def column_states(coeff, main_table, spot, row, slots):
    sources, rows, _ = coeff.shape
    cols, depth = main_table.shape
    total = slots * LANES
    whole = lambda x: pl.BlockSpec(x.shape, lambda v: (0,) * x.ndim)
    return pl.pallas_call(
        state_kernel,
        out_shape=jax.ShapeDtypeStruct((total, 5 * LANES), BF16),
        grid=(4,),
        in_specs=[
            whole(main_table),
            whole(spot),
            whole(row),
            pl.BlockSpec((sources, rows // 4, LANES), lambda v: (0, v, 0)),
        ],
        out_specs=pl.BlockSpec((total, 5 * LANES), lambda v: (0, 0)),
        scratch_shapes=[
            pltpu.VMEM((depth, 4 * LANES), BF16),
            pltpu.VMEM((2 * depth, LANES), F32),
            pltpu.VMEM((sources * 2 * 16, LANES), F32),
            pltpu.VMEM((cols, 5 * LANES), BF16),
        ],
        compiler_params=pltpu.CompilerParams(vmem_limit_bytes=28 << 20),
        name="states",
    )(main_table, spot, row, coeff)


def jacobian_kernel(jac_ref, bias_ref, out_ref):
    channels = jac_ref.shape[1]
    levels = jac_ref.shape[0] // 4
    jac = jac_ref[...].astype(F32)
    out_ref[...] = jnp.zeros_like(out_ref)
    for v in range(4):
        at = v * levels
        out_ref[v * LANES : (v + 1) * LANES, :] = jac[at : at + LANES].astype(BF16)
        lo = 4 * LANES + (v % 2 * 2 + v // 2) * SLOT_LANES
        pad = jnp.zeros((16 - (levels - LANES), channels), F32)
        piece = jnp.concatenate([jac[at + LANES : at + levels], pad], axis=0)
        out_ref[lo : lo + 16, :] = piece.astype(BF16)
    parts = []
    left = bias_ref[...]
    for _ in range(3):
        parts.append(left.astype(BF16).astype(F32))
        left = left - parts[-1]
    parts.append(jnp.zeros((13, channels), F32))
    out_ref[5 * LANES :, :] = jnp.concatenate(parts, axis=0).astype(BF16)


def owner_table(jac_t, bias):
    return pl.pallas_call(
        jacobian_kernel,
        out_shape=jax.ShapeDtypeStruct((5 * LANES + 16, jac_t.shape[1]), BF16),
        compiler_params=pltpu.CompilerParams(vmem_limit_bytes=16 << 20),
        name="jacobians",
    )(jac_t, bias)


def answer_kernel(core_ref, state_ref, own_ref, other_ref, out_ref):
    width = 5 * LANES
    sources = state_ref.shape[0]
    rows = sources * 8
    first = core_ref[0] == 0
    states = state_ref[...].astype(F32)
    low, high = states[:, :8].reshape(rows, width), states[:, 8:].reshape(rows, width)

    def answer(state, jac_ref):
        bias = jnp.sum(jac_ref[width:, :].astype(F32), axis=0, keepdims=True)
        depart = dot(state.astype(BF16), jac_ref[:width, :]) + bias
        weighted = (depart / jnp.sqrt(1.0 + depart * depart * 0.25)).astype(BF16)
        grad = lax.dot_general(
            weighted, jac_ref[:width, :], (((1,), (1,)), ((), ())), preferred_element_type=F32
        )
        return depart, grad

    own = answer(jnp.where(first, low, high), own_ref)
    other = answer(jnp.where(first, high, low), other_ref)
    for part, at in ((0, 0), (1, 3 * LANES)):
        size = own[part].shape[1]
        low = jnp.where(first, own[part], other[part]).reshape(sources, 8, size)
        high = jnp.where(first, other[part], own[part]).reshape(sources, 8, size)
        both = jnp.concatenate([low, high], axis=1)
        out_ref[:, :, at : at + size] = both.astype(BF16)


def answers(states, core, own, other):
    sources, rows, width = states.shape
    steps = 2
    return pl.pallas_call(
        answer_kernel,
        out_shape=jax.ShapeDtypeStruct((sources, rows, 8 * LANES), BF16),
        grid=(steps,),
        in_specs=[
            pl.BlockSpec(memory_space=pltpu.SMEM),
            pl.BlockSpec((sources // steps, rows, width), lambda g: (g, 0, 0)),
            pl.BlockSpec(own.shape, lambda g: (0, 0)),
            pl.BlockSpec(own.shape, lambda g: (0, 0)),
        ],
        out_specs=pl.BlockSpec((sources // steps, rows, 8 * LANES), lambda g: (g, 0, 0)),
        compiler_params=pltpu.CompilerParams(vmem_limit_bytes=20 << 20),
        name="answers",
    )(core, states, own, other)


def collect_kernel(spot_ref, back_ref, depart_ref, grad_ref):
    cols = spot_ref.shape[1]
    total = back_ref.shape[0]
    spot = jnp.transpose(jnp.broadcast_to(spot_ref[...].astype(F32), (LANES, cols)))[:, :1]
    place = lax.broadcasted_iota(jnp.int32, (cols, total), 1) == spot.astype(jnp.int32)
    place = jnp.where(place, 1.0, 0.0).astype(BF16)
    channels = depart_ref.shape[0]
    width = grad_ref.shape[0]
    both = jnp.transpose(dot(place, back_ref[...]))
    depart_ref[...] = both[:channels].astype(BF16)
    levels = width // 4
    parts = []
    for v in range(4):
        lo = 7 * LANES + (v % 2 * 2 + v // 2) * SLOT_LANES
        parts.append(both[(3 + v) * LANES : (4 + v) * LANES])
        parts.append(both[lo : lo + levels - LANES])
    grad_ref[...] = jnp.concatenate(parts, axis=0).astype(BF16)


def collect(spot, back, channels, width):
    cols = spot.shape[1]
    return pl.pallas_call(
        collect_kernel,
        out_shape=(
            jax.ShapeDtypeStruct((channels, cols), BF16),
            jax.ShapeDtypeStruct((width, cols), BF16),
        ),
        compiler_params=pltpu.CompilerParams(vmem_limit_bytes=20 << 20),
        name="collect",
    )(spot, back)


def exchange(x, axes):
    return lax.all_to_all(x, axes, split_axis=0, concat_axis=0, tiled=True)


def local(control, spread, vertical, legendre, column_index, column_owner, jacobian, channel_bias):
    pairs = control.shape[0]
    wave_count = lax.axis_size("wave")
    device_count = wave_count * lax.axis_size("z") * lax.axis_size("core")
    cols = column_index.shape[0]
    slots = max(2, 2 * cols // device_count)
    var = lax.axis_index("z")
    pair_base = (lax.axis_index("wave") * pairs).astype(jnp.int32).reshape(1)
    blocks = fourier_blocks(control, spread[var], vertical[var], legendre, pair_base, device_count)
    index = column_index.reshape(1, cols)
    main_table, row, spot = tables(
        index, column_owner.reshape(1, cols), 4 * pairs * wave_count, slots
    )
    jac_t = jnp.transpose(jacobian[0])
    own = owner_table(jac_t, channel_bias)
    other = lax.ppermute(own, "core", [(0, 1), (1, 0)])
    coeff = exchange(blocks, ("wave", "z", "core")).reshape(wave_count, -1, LANES)
    outgoing = column_states(coeff, main_table, spot, row, slots)
    chips = device_count // 2
    states = exchange(outgoing.reshape(chips, 2 * slots, outgoing.shape[1]), ("wave", "z"))
    core = lax.axis_index("core").astype(jnp.int32).reshape(1)
    back = exchange(answers(states, core, own, other), ("wave", "z"))
    departures, increments = collect(
        spot, back.reshape(device_count * slots, -1), jac_t.shape[1], jac_t.shape[0]
    )
    return (jnp.transpose(departures), jnp.transpose(increments))


def solution(mesh):
    waves, lats = mesh.devices.shape
    split = Mesh(mesh.devices.reshape(waves, lats // 2, 2), ("wave", "z", "core"))
    lat = ("z", "core")
    everyone = ("wave", "z", "core")
    return jax.shard_map(
        local,
        mesh=split,
        in_specs=(
            P("wave", None, lat, None),
            P(),
            P(),
            P("wave", None, None),
            P(everyone),
            P(everyone, None),
            P(everyone, None, None),
            P(everyone, None),
        ),
        out_specs=(P(everyone, None), P(everyone, None)),
        check_vma=False,
    )
```

```python
import functools
import math

import jax
import jax.numpy as jnp
from jax import lax
from jax.experimental import pallas as pl
from jax.experimental.pallas import tpu as pltpu
from jax.sharding import PartitionSpec as P

NLON = 2560
LANES = 128
SLOT_LANES = 32
REST = 12
GROUP = 10
F32 = jnp.float32
BF16 = jnp.bfloat16


def dot(a, b):
    return jnp.dot(a, b, preferred_element_type=F32)


def fourier_kernel(
    base_ref,
    ctrl_ref,
    spread_ref,
    vert_ref,
    leg_ref,
    out_ref,
    main_s,
    rest_s,
    rem_s,
    leg_s,
    leg_sem,
    spread_s,
    second_s,
    first_s,
    scaled_s,
    spec_s,
    vert_s,
):
    slots = ctrl_ref.shape[3]
    waves = slots - 1
    modes = ctrl_ref.shape[2]
    rows = leg_ref.shape[2]
    dests = out_ref.shape[0]
    steps = pl.num_programs(0) - 3
    depth = leg_s.shape[0]
    t = pl.program_id(0)
    lane = lax.broadcasted_iota(jnp.int32, (1, LANES), 1)
    slot = lax.broadcasted_iota(jnp.int32, (1, slots), 1)

    def fetch(step):
        at = step % depth
        return pltpu.make_async_copy(
            leg_ref.at[pl.ds(4 * step, 4)], leg_s.at[at], leg_sem.at[at]
        )

    def align(step):
        pair = base_ref[0] + step * 4
        skip = pair // LANES
        shift = pair - skip * LANES
        last = None
        for k in range(6):
            if last is None:
                last = pltpu.roll(
                    spread_s[:, pl.ds(pl.multiple_of(skip * LANES, LANES), LANES)], LANES - shift, 1
                )
            after = spread_s[:, pl.ds(pl.multiple_of((skip + k + 1) * LANES, LANES), LANES)]
            after = pltpu.roll(after, LANES - shift, 1)
            first_s[:, k * LANES : (k + 1) * LANES] = jnp.where(lane < LANES - shift, last, after)
            last = after

    def scale(step, i):
        pair = base_ref[0] + step * 4 + i
        last = first_s[:, :LANES]
        last = pltpu.roll(last, LANES - i, 1) if i else last
        for k in range(5):
            at = slice(k * LANES, (k + 1) * LANES)
            after = first_s[:, (k + 1) * LANES : (k + 2) * LANES]
            after = pltpu.roll(after, LANES - i, 1) if i else after
            factor = jnp.where(lane < LANES - i, last, after) if i else last
            last = after
            if k >= 2:
                factor = jnp.where(lane + k * LANES < waves - pair, factor, second_s[:, at])
            scaled_s[:, at] = (ctrl_ref[i, 0, :, at].astype(F32) * factor).astype(BF16)
        end = ctrl_ref[i, 0, :, waves:].astype(F32) * second_s[:, waves : waves + 1]
        scaled_s[:, waves : waves + 1] = end.astype(BF16)
        spec_s[i] = dot(vert_s[...], scaled_s[:, :slots]).astype(BF16)

    def sums(step, i, early):
        pair = base_ref[0] + step * 4 + i
        spec = spec_s[i]
        lo, hi = (512, slots) if early else (256, 512)
        mixed = spec[:, lo:hi]
        keep = slot[:, lo:hi] < waves - pair
        zero = jnp.zeros_like(mixed)
        both = jnp.concatenate(
            [jnp.where(keep, mixed, zero), jnp.where(keep, zero, mixed)], axis=0
        )
        both = dot(both, leg_s[(t - 1) % depth, i, lo:hi, :])
        half_rows = spec.shape[0]
        first = both[:half_rows] + dot(spec[:, :lo], leg_s[(t - 1) % depth, i, :lo, :])
        second = both[half_rows:]
        if not early:
            second = second + dot(spec[:, hi:], leg_s[(t - 1) % depth, i, hi:, :])
        parts = (first, second)
        for h in range(2):
            j = 2 * i + h
            main_s[pl.ds(j, rows, stride=8), :] = jnp.transpose(parts[h][:LANES])
            rest_s[step, 16 * j : 16 * j + 16, :] = parts[h][LANES:]

    def emit():
        out_ref[...] = main_s[...].reshape(dests, 32, LANES).astype(BF16)

    @pl.when(t == 0)
    def _():
        for step in range(depth):
            fetch(step).start()
        mine = lax.broadcasted_iota(jnp.int32, (1, 4, 1), 1) == base_ref[1]
        spread = jnp.sum(jnp.where(mine, spread_ref[...], 0.0), axis=1)
        spread_s[:, waves:] = jnp.zeros((modes, spread_s.shape[1] - waves), F32)
        spread_s[:, :waves] = spread
        second_s[:, :waves] = pltpu.roll(spread, 1, 1)
        second_s[:, waves : waves + 1] = spread[:, waves - 1 :]
        vert = jnp.sum(jnp.where(mine, vert_ref[...].astype(F32), 0.0), axis=1)
        vert_s[...] = jnp.zeros_like(vert_s)
        vert_s[:modes, :] = vert.astype(BF16)
        rem_s[...] = jnp.zeros_like(rem_s)
        align(0)
        for i in range(4):
            scale(0, i)

    @pl.when((t > 0) & (t <= steps))
    def _():
        fetch(t - 1).wait()

    @pl.when((t > 1) & (t - 2 + depth < steps))
    def _():
        fetch(t - 2 + depth).start()

    for early in (True, False):

        @pl.when((t > 0) & (t <= steps) & ((base_ref[0] + 4 * t <= 128) == early))
        def _():
            emit()
            align(jnp.minimum(t, steps - 1))
            for i in range(4):
                sums(t - 1, i, early)
                scale(jnp.minimum(t, steps - 1), i)

    @pl.when(t == steps + 1)
    def _():
        emit()

    @pl.when(t == steps + 2)
    def _():
        for k in range(8 * steps):
            at = LANES * (k // GROUP) + REST * (k % GROUP)
            lo = 16 * (k % 8)
            rem_s[at : at + REST, :] = rest_s[k // 8, lo : lo + REST, :]
        for u in range(4):
            main_s[pl.ds(u, rows, stride=4), :] = jnp.transpose(rem_s[u * LANES : (u + 1) * LANES])
        out_ref[:, :16, :] = main_s[: 4 * rows, :].reshape(dests, 16, LANES).astype(BF16)


def fourier_blocks(control, spread, vertical, legendre, base, dests):
    pairs, slots, _, modes = control.shape
    rows = legendre.shape[2]
    ctrl = jnp.transpose(control, (0, 2, 3, 1))
    steps = pairs // 4
    return pl.pallas_call(
        fourier_kernel,
        out_shape=jax.ShapeDtypeStruct((dests, 32 * steps + 16, LANES), BF16),
        grid=(steps + 3,),
        in_specs=[
            pl.BlockSpec(memory_space=pltpu.SMEM),
            pl.BlockSpec((4, 1, modes, slots), lambda t: (jnp.minimum(t, steps - 1), 0, 0, 0)),
            pl.BlockSpec((modes, 4, slots - 1), lambda t: (0, 0, 0)),
            pl.BlockSpec((modes, 4, modes), lambda t: (0, 0, 0)),
            pl.BlockSpec(memory_space=pl.ANY),
        ],
        out_specs=pl.BlockSpec((dests, 32, LANES), lambda t: (0, jnp.maximum(t - 2, 0), 0)),
        scratch_shapes=[
            pltpu.VMEM((rows * 8, LANES), F32),
            pltpu.VMEM((steps, LANES, rows), F32),
            pltpu.VMEM((4 * LANES, rows), F32),
            pltpu.VMEM((3, 4, slots, rows), BF16),
            pltpu.SemaphoreType.DMA((3,)),
            pltpu.VMEM((modes, 9 * LANES), F32),
            pltpu.VMEM((modes, 6 * LANES), F32),
            pltpu.VMEM((modes, 6 * LANES), F32),
            pltpu.VMEM((modes, 6 * LANES), BF16),
            pltpu.VMEM((4, 144, slots), BF16),
            pltpu.VMEM((144, modes), BF16),
        ],
        name="fourier",
    )(
        base,
        ctrl,
        jnp.transpose(spread, (2, 0, 1)),
        jnp.transpose(vertical, (1, 0, 2)),
        legendre,
    )


def cosine(turns):
    x = turns * math.pi
    y = x * x
    s = -1.0 / 39916800.0
    for c in (1.0 / 362880.0, -1.0 / 5040.0, 1.0 / 120.0, -1.0 / 6.0, 1.0):
        s = s * y + c
    s = s * x
    return 1.0 - 2.0 * (s * s)


def table_kernel(slots, index_ref, owner_ref, main_ref, row_ref, spot_ref):
    cols = index_ref.shape[1]
    depth = main_ref.shape[1]
    waves = depth // 2
    column = jnp.transpose(jnp.broadcast_to(index_ref[...].astype(F32), (LANES, cols)))
    row = jnp.floor((column + 0.5) * (1.0 / NLON))
    row_ref[...] = row
    column = column[:, :1]
    row = row[:, :1]
    longitude = column - row * NLON
    lane = lax.broadcasted_iota(jnp.int32, (1, depth), 1)

    source = lane // 80
    part = lane % 80 // 40
    local = lane % 40
    pair = source * 20 + local // 2
    wave = jnp.where(local % 2 == 0, pair, waves - 1 - pair)
    weight = jnp.where(wave == 0, 1.0, 2.0).astype(F32)
    wave_f = wave.astype(F32)
    shift = part.astype(F32) * (NLON // 4)
    for c in range(0, cols, 64):
        turns = longitude[c : c + 64] * wave_f + shift
        turns = turns - jnp.floor(turns * (1.0 / NLON) + 0.5) * NLON
        main_ref[c : c + 64, :] = (weight * cosine(turns * (1.0 / NLON))).astype(BF16)

    hits = lax.broadcasted_iota(jnp.int32, (LANES, cols), 0) == owner_ref[...]
    hits_f = jnp.where(hits, 1.0, 0.0).astype(F32)
    before = (
        lax.broadcasted_iota(jnp.int32, (cols, cols), 0)
        < lax.broadcasted_iota(jnp.int32, (cols, cols), 1)
    )
    earlier = dot(hits_f.astype(BF16), jnp.where(before, 1.0, 0.0).astype(BF16))
    first = (lax.broadcasted_iota(jnp.int32, (LANES, cols), 0) * slots).astype(F32)
    spot = jnp.sum(hits_f * (first + earlier), axis=0, keepdims=True).astype(jnp.int32)
    spot_ref[...] = spot


def tables(index, owner, depth, slots):
    cols = index.shape[1]
    return pl.pallas_call(
        functools.partial(table_kernel, slots),
        out_shape=(
            jax.ShapeDtypeStruct((cols, depth), BF16),
            jax.ShapeDtypeStruct((cols, LANES), F32),
            jax.ShapeDtypeStruct((1, cols), jnp.int32),
        ),
        cost_estimate=pl.CostEstimate(
            flops=60 * cols * depth, bytes_accessed=4 << 20, transcendentals=0
        ),
        compiler_params=pltpu.CompilerParams(vmem_limit_bytes=24 << 20),
        name="tables",
    )(index, owner)


def state_kernel(
    main_ref, spot_ref, row_ref, coeff_ref, out_ref, coeff_s, tail_s, take_s, state_s
):
    v = pl.program_id(0)
    cols = main_ref.shape[0]
    depth = main_ref.shape[1]
    sources = coeff_ref.shape[0]
    block = coeff_ref[...].astype(F32).reshape(sources * 2, 22, 8, LANES)
    for r in range(4):
        picked = jnp.stack([block[:, 4 * g + r] for g in range(5)], axis=1)
        coeff_s[:, r * LANES : (r + 1) * LANES] = picked.reshape(depth, LANES).astype(BF16)
    take_s[...] = block[:, 20:].reshape(sources * 2 * 16, LANES)
    lane = lax.broadcasted_iota(jnp.int32, (1, LANES), 1)
    odd = v % 2
    for u in range(4):
        picked = [take_s[pl.ds(4 * r + u, sources * 2, stride=16), :] for r in range(4)]
        for k in range(GROUP):
            at = pl.ds(v // 2 * depth + u * GROUP + k, sources * 2, stride=4 * GROUP)
            kept = tail_s[at, :]
            for r in range(4):
                moved = pltpu.roll(picked[r], (64 * odd + 16 * r - REST * k + LANES) % LANES, 1)
                kept = jnp.where(lane // 16 == 4 * odd + r, moved, kept)
            tail_s[at, :] = kept
    row = row_ref[...]
    products = dot(main_ref[...], coeff_s[...])
    main = products[:, :LANES]
    for r in range(1, 4):
        main = jnp.where(row == r, products[:, r * LANES : (r + 1) * LANES], main)
    state_s[:, pl.ds(pl.multiple_of(v * LANES, LANES), LANES)] = main.astype(BF16)

    @pl.when(v == pl.num_programs(0) - 1)
    def _():
        wide = jnp.concatenate([tail_s[:depth], tail_s[depth:]], axis=1)
        products = dot(main_ref[...], wide.astype(BF16))
        folded = []
        for half in range(2):
            part = products[:, half * LANES : (half + 1) * LANES]
            part = jnp.where((lane // 16 % 4).astype(F32) == row, part, 0.0)
            part = part + pltpu.roll(part, LANES - 32, 1)
            folded.append(part + pltpu.roll(part, LANES - 16, 1))
        tail = jnp.where(lane % 64 < 32, folded[0], pltpu.roll(folded[1], 32, 1))
        state_s[:, 4 * LANES :] = jnp.where(lane % 32 < 9, tail, 0.0).astype(BF16)
        place = lax.broadcasted_iota(jnp.int32, (out_ref.shape[0], cols), 0) == spot_ref[...]
        place = jnp.where(place, 1.0, 0.0).astype(BF16)
        out_ref[...] = dot(place, state_s[...]).astype(BF16)


def column_states(coeff, main_table, spot, row, slots):
    sources, rows, _ = coeff.shape
    cols, depth = main_table.shape
    total = slots * LANES
    whole = lambda x: pl.BlockSpec(x.shape, lambda v: (0,) * x.ndim)
    return pl.pallas_call(
        state_kernel,
        out_shape=jax.ShapeDtypeStruct((total, 5 * LANES), BF16),
        grid=(4,),
        in_specs=[
            whole(main_table),
            whole(spot),
            whole(row),
            pl.BlockSpec((sources, rows // 4, LANES), lambda v: (0, v, 0)),
        ],
        out_specs=pl.BlockSpec((total, 5 * LANES), lambda v: (0, 0)),
        scratch_shapes=[
            pltpu.VMEM((depth, 4 * LANES), BF16),
            pltpu.VMEM((2 * depth, LANES), F32),
            pltpu.VMEM((sources * 2 * 16, LANES), F32),
            pltpu.VMEM((cols, 5 * LANES), BF16),
        ],
        compiler_params=pltpu.CompilerParams(vmem_limit_bytes=28 << 20),
        name="states",
    )(main_table, spot, row, coeff)


def answer_kernel(state_ref, jac_ref, bias_ref, out_ref, jac_s):
    channels = jac_ref.shape[1]
    levels = jac_ref.shape[0] // 4
    rest = levels - LANES

    @pl.when(pl.program_id(0) == 0)
    def _():
        jac = jac_ref[...].astype(F32)
        jac_s[...] = jnp.zeros_like(jac_s)
        for v in range(4):
            at = v * levels
            jac_s[v * LANES : (v + 1) * LANES, :] = jac[at : at + LANES].astype(BF16)
            lo = 4 * LANES + (v % 2 * 2 + v // 2) * SLOT_LANES
            piece = jnp.concatenate(
                [jac[at + LANES : at + levels], jnp.zeros((16 - rest, channels), F32)], axis=0
            )
            jac_s[lo : lo + 16, :] = piece.astype(BF16)

    depart = dot(state_ref[...], jac_s[...]) + bias_ref[...]
    weighted = (depart / jnp.sqrt(1.0 + depart * depart * 0.25)).astype(BF16)
    out_ref[:, :channels] = depart.astype(BF16)
    out_ref[:, 3 * LANES : 3 * LANES + jac_ref.shape[0]] = lax.dot_general(
        weighted, jac_ref[...], (((1,), (1,)), ((), ())), preferred_element_type=F32
    ).astype(BF16)


def answers(states, jac_t, bias):
    total, lanes = states.shape
    width, channels = jac_t.shape
    out_lanes = -(-channels // LANES) * LANES + -(-width // LANES) * LANES
    steps = 2
    return pl.pallas_call(
        answer_kernel,
        out_shape=jax.ShapeDtypeStruct((total, out_lanes), BF16),
        grid=(steps,),
        in_specs=[
            pl.BlockSpec((total // steps, lanes), lambda g: (g, 0)),
            pl.BlockSpec((width, channels), lambda g: (0, 0)),
            pl.BlockSpec((1, channels), lambda g: (0, 0)),
        ],
        out_specs=pl.BlockSpec((total // steps, out_lanes), lambda g: (g, 0)),
        scratch_shapes=[pltpu.VMEM((lanes, channels), BF16)],
        compiler_params=pltpu.CompilerParams(vmem_limit_bytes=20 << 20),
        name="answers",
    )(states, jac_t, bias)


def collect_kernel(spot_ref, back_ref, depart_ref, grad_ref):
    cols = spot_ref.shape[1]
    total = back_ref.shape[0]
    spot = jnp.transpose(jnp.broadcast_to(spot_ref[...].astype(F32), (LANES, cols)))[:, :1]
    place = lax.broadcasted_iota(jnp.int32, (cols, total), 1) == spot.astype(jnp.int32)
    place = jnp.where(place, 1.0, 0.0).astype(BF16)
    channels = depart_ref.shape[0]
    width = grad_ref.shape[0]
    both = jnp.transpose(dot(place, back_ref[...]))
    depart_ref[...] = both[:channels].astype(BF16)
    grad_ref[...] = both[3 * LANES : 3 * LANES + width].astype(BF16)


def collect(spot, back, channels, width):
    cols = spot.shape[1]
    return pl.pallas_call(
        collect_kernel,
        out_shape=(
            jax.ShapeDtypeStruct((channels, cols), BF16),
            jax.ShapeDtypeStruct((width, cols), BF16),
        ),
        compiler_params=pltpu.CompilerParams(vmem_limit_bytes=20 << 20),
        name="collect",
    )(spot, back)


def exchange(x):
    return lax.all_to_all(x, ("wave", "lat"), split_axis=0, concat_axis=0, tiled=True)


def local(control, spread, vertical, legendre, column_index, column_owner, jacobian, channel_bias):
    pairs = control.shape[0]
    wave_count = lax.axis_size("wave")
    device_count = wave_count * lax.axis_size("lat")
    cols = column_index.shape[0]
    slots = max(2, 2 * cols // device_count)
    base = jnp.stack([lax.axis_index("wave") * pairs, lax.axis_index("lat") // 2])
    blocks = fourier_blocks(
        control, spread, vertical, legendre, base.astype(jnp.int32), device_count
    )
    index = column_index.reshape(1, cols)
    main_table, row, spot = tables(
        index, column_owner.reshape(1, cols), 4 * pairs * wave_count, slots
    )
    coeff = exchange(blocks).reshape(wave_count, -1, LANES)
    outgoing = column_states(coeff, main_table, spot, row, slots)
    lanes = outgoing.shape[1]
    states = exchange(outgoing.reshape(device_count, slots, lanes))
    jac_t = jnp.transpose(jacobian[0])
    reply = answers(states.reshape(device_count * slots, lanes), jac_t, channel_bias)
    back = exchange(reply.reshape(device_count, slots, reply.shape[1]))
    departures, increments = collect(
        spot, back.reshape(device_count * slots, -1), jac_t.shape[1], jac_t.shape[0]
    )
    return (jnp.transpose(departures), jnp.transpose(increments))


def solution(mesh):
    return jax.shard_map(
        local,
        mesh=mesh,
        in_specs=(
            P("wave", None, "lat", None),
            P(),
            P(),
            P("wave", None, None),
            P(("wave", "lat")),
            P(("wave", "lat"), None),
            P(("wave", "lat"), None, None),
            P(("wave", "lat"), None),
        ),
        out_specs=(P(("wave", "lat"), None), P(("wave", "lat"), None)),
        check_vma=False,
    )
```

```python
import functools
import math

import jax
import jax.numpy as jnp
from jax import lax
from jax.experimental import pallas as pl
from jax.experimental.pallas import tpu as pltpu
from jax.sharding import PartitionSpec as P

NLON = 2560
LANES = 128
SLOT_LANES = 32
REST = 12
GROUP = 10
F32 = jnp.float32
BF16 = jnp.bfloat16


def dot(a, b):
    return jnp.dot(a, b, preferred_element_type=F32)


def fourier_kernel(
    base_ref,
    var_ref,
    ctrl_ref,
    spread_ref,
    vert_ref,
    leg_ref,
    out_ref,
    main_s,
    rest_s,
    rem_s,
    leg_s,
    leg_sem,
    spread_s,
    second_s,
    first_s,
    scaled_s,
    spec_s,
    vert_s,
    wide_s,
):
    slots = ctrl_ref.shape[3]
    waves = slots - 1
    modes = ctrl_ref.shape[2]
    rows = leg_ref.shape[2]
    dests = out_ref.shape[0]
    steps = pl.num_programs(0) - 3
    depth = leg_s.shape[0]
    t = pl.program_id(0)
    lane = lax.broadcasted_iota(jnp.int32, (1, LANES), 1)
    slot = lax.broadcasted_iota(jnp.int32, (1, slots), 1)

    def fetch(step):
        at = step % depth
        return pltpu.make_async_copy(
            leg_ref.at[pl.ds(4 * step, 4)], leg_s.at[at], leg_sem.at[at]
        )

    def align(step):
        pair = base_ref[0] + step * 4
        skip = pair // LANES
        shift = pair - skip * LANES
        last = None
        for k in range(6):
            if last is None:
                last = pltpu.roll(
                    spread_s[:, pl.ds(pl.multiple_of(skip * LANES, LANES), LANES)], LANES - shift, 1
                )
            after = spread_s[:, pl.ds(pl.multiple_of((skip + k + 1) * LANES, LANES), LANES)]
            after = pltpu.roll(after, LANES - shift, 1)
            first_s[:, k * LANES : (k + 1) * LANES] = jnp.where(lane < LANES - shift, last, after)
            last = after

    def scale(step, i):
        pair = base_ref[0] + step * 4 + i
        last = first_s[:, :LANES]
        last = pltpu.roll(last, LANES - i, 1) if i else last
        for k in range(5):
            at = slice(k * LANES, (k + 1) * LANES)
            after = first_s[:, (k + 1) * LANES : (k + 2) * LANES]
            after = pltpu.roll(after, LANES - i, 1) if i else after
            factor = jnp.where(lane < LANES - i, last, after) if i else last
            last = after
            if k >= 2:
                factor = jnp.where(lane + k * LANES < waves - pair, factor, second_s[:, at])
            scaled_s[:, at] = (ctrl_ref[i, 0, :, at].astype(F32) * factor).astype(BF16)
        end = ctrl_ref[i, 0, :, waves:].astype(F32) * second_s[:, waves : waves + 1]
        scaled_s[:, waves : waves + 1] = end.astype(BF16)
        spec_s[i] = dot(vert_s[...], scaled_s[:, :slots]).astype(BF16)

    def sums(step, i, early):
        pair = base_ref[0] + step * 4 + i
        spec = spec_s[i]
        lo, hi = (512, slots) if early else (256, 512)
        mixed = spec[:, lo:hi]
        keep = slot[:, lo:hi] < waves - pair
        zero = jnp.zeros_like(mixed)
        both = jnp.concatenate(
            [jnp.where(keep, mixed, zero), jnp.where(keep, zero, mixed)], axis=0
        )
        both = dot(both, leg_s[(t - 1) % depth, i, lo:hi, :])
        half_rows = spec.shape[0]
        first = both[:half_rows] + dot(spec[:, :lo], leg_s[(t - 1) % depth, i, :lo, :])
        second = both[half_rows:]
        if not early:
            second = second + dot(spec[:, hi:], leg_s[(t - 1) % depth, i, hi:, :])
        parts = (first, second)
        for h in range(2):
            j = 2 * i + h
            main_s[pl.ds(j, rows, stride=8), :] = jnp.transpose(parts[h][:LANES])
            rest_s[step, 16 * j : 16 * j + 16, :] = parts[h][LANES:]

    def emit():
        out_ref[...] = main_s[...].reshape(dests, 32, LANES).astype(BF16)

    @pl.when(t == 0)
    def _():
        for step in range(depth):
            fetch(step).start()
        spread = spread_ref[:, var_ref[0], :]
        spread_s[:, waves:] = jnp.zeros((modes, spread_s.shape[1] - waves), F32)
        spread_s[:, :waves] = spread
        second_s[:, :waves] = pltpu.roll(spread, 1, 1)
        second_s[:, waves : waves + 1] = spread[:, waves - 1 :]
        wide_s[...] = vert_ref[...].astype(F32)
        vert = wide_s[:, var_ref[0], :]
        vert_s[...] = jnp.zeros_like(vert_s)
        vert_s[:modes, :] = vert.astype(BF16)
        rem_s[...] = jnp.zeros_like(rem_s)
        align(0)
        for i in range(4):
            scale(0, i)

    @pl.when((t > 0) & (t <= steps))
    def _():
        fetch(t - 1).wait()

    @pl.when((t > 1) & (t - 2 + depth < steps))
    def _():
        fetch(t - 2 + depth).start()

    for early in (True, False):

        @pl.when((t > 0) & (t <= steps) & ((base_ref[0] + 4 * t <= 128) == early))
        def _():
            emit()
            align(jnp.minimum(t, steps - 1))
            for i in range(4):
                sums(t - 1, i, early)
                scale(jnp.minimum(t, steps - 1), i)

    @pl.when(t == steps + 1)
    def _():
        emit()

    @pl.when(t == steps + 2)
    def _():
        for k in range(8 * steps):
            at = LANES * (k // GROUP) + REST * (k % GROUP)
            lo = 16 * (k % 8)
            rem_s[at : at + REST, :] = rest_s[k // 8, lo : lo + REST, :]
        for u in range(4):
            main_s[pl.ds(u, rows, stride=4), :] = jnp.transpose(rem_s[u * LANES : (u + 1) * LANES])
        out_ref[:, :16, :] = main_s[: 4 * rows, :].reshape(dests, 16, LANES).astype(BF16)


def fourier_blocks(control, spread, vertical, legendre, base, var, dests):
    pairs, slots, _, modes = control.shape
    rows = legendre.shape[2]
    ctrl = jnp.transpose(control, (0, 2, 3, 1))
    steps = pairs // 4
    return pl.pallas_call(
        fourier_kernel,
        out_shape=jax.ShapeDtypeStruct((dests, 32 * steps + 16, LANES), BF16),
        grid=(steps + 3,),
        in_specs=[
            pl.BlockSpec(memory_space=pltpu.SMEM),
            pl.BlockSpec(memory_space=pltpu.SMEM),
            pl.BlockSpec((4, 1, modes, slots), lambda t: (jnp.minimum(t, steps - 1), 0, 0, 0)),
            pl.BlockSpec((modes, 4, slots - 1), lambda t: (0, 0, 0)),
            pl.BlockSpec((modes, 4, modes), lambda t: (0, 0, 0)),
            pl.BlockSpec(memory_space=pl.ANY),
        ],
        out_specs=pl.BlockSpec((dests, 32, LANES), lambda t: (0, jnp.maximum(t - 2, 0), 0)),
        scratch_shapes=[
            pltpu.VMEM((rows * 8, LANES), F32),
            pltpu.VMEM((steps, LANES, rows), F32),
            pltpu.VMEM((4 * LANES, rows), F32),
            pltpu.VMEM((3, 4, slots, rows), BF16),
            pltpu.SemaphoreType.DMA((3,)),
            pltpu.VMEM((modes, 9 * LANES), F32),
            pltpu.VMEM((modes, 6 * LANES), F32),
            pltpu.VMEM((modes, 6 * LANES), F32),
            pltpu.VMEM((modes, 6 * LANES), BF16),
            pltpu.VMEM((4, 144, slots), BF16),
            pltpu.VMEM((144, modes), BF16),
            pltpu.VMEM((modes, 4, modes), F32),
        ],
        name="fourier",
    )(
        base,
        var,
        ctrl,
        jnp.transpose(spread, (2, 0, 1)),
        jnp.transpose(vertical, (1, 0, 2)),
        legendre,
    )


def cosine(turns):
    x = turns * math.pi
    y = x * x
    s = -1.0 / 39916800.0
    for c in (1.0 / 362880.0, -1.0 / 5040.0, 1.0 / 120.0, -1.0 / 6.0, 1.0):
        s = s * y + c
    s = s * x
    return 1.0 - 2.0 * (s * s)


def table_kernel(slots, index_ref, owner_ref, main_ref, row_ref, spot_ref):
    cols = index_ref.shape[1]
    depth = main_ref.shape[1]
    waves = depth // 2
    column = jnp.transpose(jnp.broadcast_to(index_ref[...].astype(F32), (LANES, cols)))
    row = jnp.floor((column + 0.5) * (1.0 / NLON))
    row_ref[...] = row
    column = column[:, :1]
    row = row[:, :1]
    longitude = column - row * NLON
    lane = lax.broadcasted_iota(jnp.int32, (1, depth), 1)

    source = lane // 80
    part = lane % 80 // 40
    local = lane % 40
    pair = source * 20 + local // 2
    wave = jnp.where(local % 2 == 0, pair, waves - 1 - pair)
    weight = jnp.where(wave == 0, 1.0, 2.0).astype(F32)
    wave_f = wave.astype(F32)
    shift = part.astype(F32) * (NLON // 4)
    for c in range(0, cols, 64):
        turns = longitude[c : c + 64] * wave_f + shift
        turns = turns - jnp.floor(turns * (1.0 / NLON) + 0.5) * NLON
        main_ref[c : c + 64, :] = (weight * cosine(turns * (1.0 / NLON))).astype(BF16)

    hits = lax.broadcasted_iota(jnp.int32, (LANES, cols), 0) == owner_ref[...]
    hits_f = jnp.where(hits, 1.0, 0.0).astype(F32)
    before = (
        lax.broadcasted_iota(jnp.int32, (cols, cols), 0)
        < lax.broadcasted_iota(jnp.int32, (cols, cols), 1)
    )
    earlier = dot(hits_f.astype(BF16), jnp.where(before, 1.0, 0.0).astype(BF16))
    first = (lax.broadcasted_iota(jnp.int32, (LANES, cols), 0) * slots).astype(F32)
    spot = jnp.sum(hits_f * (first + earlier), axis=0, keepdims=True).astype(jnp.int32)
    spot_ref[...] = spot


def tables(index, owner, depth, slots):
    cols = index.shape[1]
    return pl.pallas_call(
        functools.partial(table_kernel, slots),
        out_shape=(
            jax.ShapeDtypeStruct((cols, depth), BF16),
            jax.ShapeDtypeStruct((cols, LANES), F32),
            jax.ShapeDtypeStruct((1, cols), jnp.int32),
        ),
        cost_estimate=pl.CostEstimate(
            flops=60 * cols * depth, bytes_accessed=4 << 20, transcendentals=0
        ),
        compiler_params=pltpu.CompilerParams(vmem_limit_bytes=24 << 20),
        name="tables",
    )(index, owner)


def state_kernel(
    main_ref, spot_ref, row_ref, coeff_ref, out_ref, coeff_s, tail_s, take_s, state_s
):
    v = pl.program_id(0)
    cols = main_ref.shape[0]
    depth = main_ref.shape[1]
    sources = coeff_ref.shape[0]
    block = coeff_ref[...].astype(F32).reshape(sources * 2, 22, 8, LANES)
    for r in range(4):
        picked = jnp.stack([block[:, 4 * g + r] for g in range(5)], axis=1)
        coeff_s[:, r * LANES : (r + 1) * LANES] = picked.reshape(depth, LANES).astype(BF16)
    take_s[...] = block[:, 20:].reshape(sources * 2 * 16, LANES)
    lane = lax.broadcasted_iota(jnp.int32, (1, LANES), 1)
    odd = v % 2
    for u in range(4):
        picked = [take_s[pl.ds(4 * r + u, sources * 2, stride=16), :] for r in range(4)]
        for k in range(GROUP):
            at = pl.ds(v // 2 * depth + u * GROUP + k, sources * 2, stride=4 * GROUP)
            kept = tail_s[at, :]
            for r in range(4):
                moved = pltpu.roll(picked[r], (64 * odd + 16 * r - REST * k + LANES) % LANES, 1)
                kept = jnp.where(lane // 16 == 4 * odd + r, moved, kept)
            tail_s[at, :] = kept
    row = row_ref[...]
    products = dot(main_ref[...], coeff_s[...])
    main = products[:, :LANES]
    for r in range(1, 4):
        main = jnp.where(row == r, products[:, r * LANES : (r + 1) * LANES], main)
    state_s[:, pl.ds(pl.multiple_of(v * LANES, LANES), LANES)] = main.astype(BF16)

    @pl.when(v == pl.num_programs(0) - 1)
    def _():
        wide = jnp.concatenate([tail_s[:depth], tail_s[depth:]], axis=1)
        products = dot(main_ref[...], wide.astype(BF16))
        folded = []
        for half in range(2):
            part = products[:, half * LANES : (half + 1) * LANES]
            part = jnp.where((lane // 16 % 4).astype(F32) == row, part, 0.0)
            part = part + pltpu.roll(part, LANES - 32, 1)
            folded.append(part + pltpu.roll(part, LANES - 16, 1))
        tail = jnp.where(lane % 64 < 32, folded[0], pltpu.roll(folded[1], 32, 1))
        state_s[:, 4 * LANES :] = jnp.where(lane % 32 < 9, tail, 0.0).astype(BF16)
        place = lax.broadcasted_iota(jnp.int32, (out_ref.shape[0], cols), 0) == spot_ref[...]
        place = jnp.where(place, 1.0, 0.0).astype(BF16)
        out_ref[...] = dot(place, state_s[...]).astype(BF16)


def column_states(coeff, main_table, spot, row, slots):
    sources, rows, _ = coeff.shape
    cols, depth = main_table.shape
    total = slots * LANES
    whole = lambda x: pl.BlockSpec(x.shape, lambda v: (0,) * x.ndim)
    return pl.pallas_call(
        state_kernel,
        out_shape=jax.ShapeDtypeStruct((total, 5 * LANES), BF16),
        grid=(4,),
        in_specs=[
            whole(main_table),
            whole(spot),
            whole(row),
            pl.BlockSpec((sources, rows // 4, LANES), lambda v: (0, v, 0)),
        ],
        out_specs=pl.BlockSpec((total, 5 * LANES), lambda v: (0, 0)),
        scratch_shapes=[
            pltpu.VMEM((depth, 4 * LANES), BF16),
            pltpu.VMEM((2 * depth, LANES), F32),
            pltpu.VMEM((sources * 2 * 16, LANES), F32),
            pltpu.VMEM((cols, 5 * LANES), BF16),
        ],
        compiler_params=pltpu.CompilerParams(vmem_limit_bytes=28 << 20),
        name="states",
    )(main_table, spot, row, coeff)


def answer_kernel(state_ref, jac_ref, bias_ref, out_ref, jac_s):
    channels = jac_ref.shape[1]
    levels = jac_ref.shape[0] // 4
    rest = levels - LANES

    @pl.when(pl.program_id(0) == 0)
    def _():
        jac = jac_ref[...].astype(F32)
        jac_s[...] = jnp.zeros_like(jac_s)
        for v in range(4):
            at = v * levels
            jac_s[v * LANES : (v + 1) * LANES, :] = jac[at : at + LANES].astype(BF16)
            lo = 4 * LANES + (v % 2 * 2 + v // 2) * SLOT_LANES
            piece = jnp.concatenate(
                [jac[at + LANES : at + levels], jnp.zeros((16 - rest, channels), F32)], axis=0
            )
            jac_s[lo : lo + 16, :] = piece.astype(BF16)

    depart = dot(state_ref[...], jac_s[...]) + bias_ref[...]
    weighted = (depart / jnp.sqrt(1.0 + depart * depart * 0.25)).astype(BF16)
    out_ref[:, :channels] = depart.astype(BF16)
    out_ref[:, 3 * LANES : 3 * LANES + jac_ref.shape[0]] = lax.dot_general(
        weighted, jac_ref[...], (((1,), (1,)), ((), ())), preferred_element_type=F32
    ).astype(BF16)


def answers(states, jac_t, bias):
    total, lanes = states.shape
    width, channels = jac_t.shape
    out_lanes = -(-channels // LANES) * LANES + -(-width // LANES) * LANES
    steps = 2
    return pl.pallas_call(
        answer_kernel,
        out_shape=jax.ShapeDtypeStruct((total, out_lanes), BF16),
        grid=(steps,),
        in_specs=[
            pl.BlockSpec((total // steps, lanes), lambda g: (g, 0)),
            pl.BlockSpec((width, channels), lambda g: (0, 0)),
            pl.BlockSpec((1, channels), lambda g: (0, 0)),
        ],
        out_specs=pl.BlockSpec((total // steps, out_lanes), lambda g: (g, 0)),
        scratch_shapes=[pltpu.VMEM((lanes, channels), BF16)],
        compiler_params=pltpu.CompilerParams(vmem_limit_bytes=20 << 20),
        name="answers",
    )(states, jac_t, bias)


def collect_kernel(spot_ref, back_ref, depart_ref, grad_ref):
    cols = spot_ref.shape[1]
    total = back_ref.shape[0]
    spot = jnp.transpose(jnp.broadcast_to(spot_ref[...].astype(F32), (LANES, cols)))[:, :1]
    place = lax.broadcasted_iota(jnp.int32, (cols, total), 1) == spot.astype(jnp.int32)
    place = jnp.where(place, 1.0, 0.0).astype(BF16)
    channels = depart_ref.shape[0]
    width = grad_ref.shape[0]
    both = jnp.transpose(dot(place, back_ref[...]))
    depart_ref[...] = both[:channels].astype(BF16)
    grad_ref[...] = both[3 * LANES : 3 * LANES + width].astype(BF16)


def collect(spot, back, channels, width):
    cols = spot.shape[1]
    return pl.pallas_call(
        collect_kernel,
        out_shape=(
            jax.ShapeDtypeStruct((channels, cols), BF16),
            jax.ShapeDtypeStruct((width, cols), BF16),
        ),
        compiler_params=pltpu.CompilerParams(vmem_limit_bytes=20 << 20),
        name="collect",
    )(spot, back)


def exchange(x):
    return lax.all_to_all(x, ("wave", "lat"), split_axis=0, concat_axis=0, tiled=True)


def local(control, spread, vertical, legendre, column_index, column_owner, jacobian, channel_bias):
    pairs = control.shape[0]
    wave_count = lax.axis_size("wave")
    device_count = wave_count * lax.axis_size("lat")
    cols = column_index.shape[0]
    slots = max(2, 2 * cols // device_count)
    base = (lax.axis_index("wave") * pairs).astype(jnp.int32).reshape(1)
    var = (lax.axis_index("lat") // 2).astype(jnp.int32).reshape(1)
    blocks = fourier_blocks(control, spread, vertical, legendre, base, var, device_count)
    index = column_index.reshape(1, cols)
    main_table, row, spot = tables(
        index, column_owner.reshape(1, cols), 4 * pairs * wave_count, slots
    )
    coeff = exchange(blocks).reshape(wave_count, -1, LANES)
    outgoing = column_states(coeff, main_table, spot, row, slots)
    lanes = outgoing.shape[1]
    states = exchange(outgoing.reshape(device_count, slots, lanes))
    jac_t = jnp.transpose(jacobian[0])
    reply = answers(states.reshape(device_count * slots, lanes), jac_t, channel_bias)
    back = exchange(reply.reshape(device_count, slots, reply.shape[1]))
    departures, increments = collect(
        spot, back.reshape(device_count * slots, -1), jac_t.shape[1], jac_t.shape[0]
    )
    return (jnp.transpose(departures), jnp.transpose(increments))


def solution(mesh):
    return jax.shard_map(
        local,
        mesh=mesh,
        in_specs=(
            P("wave", None, "lat", None),
            P(),
            P(),
            P("wave", None, None),
            P(("wave", "lat")),
            P(("wave", "lat"), None),
            P(("wave", "lat"), None, None),
            P(("wave", "lat"), None),
        ),
        out_specs=(P(("wave", "lat"), None), P(("wave", "lat"), None)),
        check_vma=False,
    )
```

```python
import functools
import math

import jax
import jax.numpy as jnp
from jax import lax
from jax.experimental import pallas as pl
from jax.experimental.pallas import tpu as pltpu
from jax.sharding import PartitionSpec as P

NLON = 2560
LANES = 128
SLOT_LANES = 32
REST = 12
GROUP = 10
F32 = jnp.float32
BF16 = jnp.bfloat16


def dot(a, b):
    return jnp.dot(a, b, preferred_element_type=F32)


def fourier_kernel(
    base_ref,
    var_ref,
    ctrl_ref,
    spread_ref,
    vert_ref,
    leg_ref,
    out_ref,
    main_s,
    rest_s,
    rem_s,
    leg_s,
    leg_sem,
    spread_s,
    second_s,
    first_s,
    scaled_s,
    spec_s,
    vert_s,
    wide_s,
):
    slots = ctrl_ref.shape[3]
    waves = slots - 1
    modes = ctrl_ref.shape[2]
    rows = leg_ref.shape[2]
    dests = out_ref.shape[0]
    steps = pl.num_programs(0) - 3
    depth = leg_s.shape[0]
    t = pl.program_id(0)
    lane = lax.broadcasted_iota(jnp.int32, (1, LANES), 1)
    slot = lax.broadcasted_iota(jnp.int32, (1, slots), 1)

    def fetch(step):
        at = step % depth
        return pltpu.make_async_copy(
            leg_ref.at[pl.ds(4 * step, 4)], leg_s.at[at], leg_sem.at[at]
        )

    def align(step):
        pair = base_ref[0] + step * 4
        skip = pair // LANES
        shift = pair - skip * LANES
        last = None
        for k in range(6):
            if last is None:
                last = pltpu.roll(
                    spread_s[:, pl.ds(pl.multiple_of(skip * LANES, LANES), LANES)], LANES - shift, 1
                )
            after = spread_s[:, pl.ds(pl.multiple_of((skip + k + 1) * LANES, LANES), LANES)]
            after = pltpu.roll(after, LANES - shift, 1)
            first_s[:, k * LANES : (k + 1) * LANES] = jnp.where(lane < LANES - shift, last, after)
            last = after

    def scale(step, i):
        pair = base_ref[0] + step * 4 + i
        last = first_s[:, :LANES]
        last = pltpu.roll(last, LANES - i, 1) if i else last
        for k in range(5):
            at = slice(k * LANES, (k + 1) * LANES)
            after = first_s[:, (k + 1) * LANES : (k + 2) * LANES]
            after = pltpu.roll(after, LANES - i, 1) if i else after
            factor = jnp.where(lane < LANES - i, last, after) if i else last
            last = after
            if k >= 2:
                factor = jnp.where(lane + k * LANES < waves - pair, factor, second_s[:, at])
            scaled_s[:, at] = (ctrl_ref[i, 0, :, at].astype(F32) * factor).astype(BF16)
        end = ctrl_ref[i, 0, :, waves:].astype(F32) * second_s[:, waves : waves + 1]
        scaled_s[:, waves : waves + 1] = end.astype(BF16)
        spec_s[i] = dot(vert_s[...], scaled_s[:, :slots]).astype(BF16)

    def sums(step, i, early):
        pair = base_ref[0] + step * 4 + i
        spec = spec_s[i]
        lo, hi = (512, slots) if early else (256, 512)
        mixed = spec[:, lo:hi]
        keep = slot[:, lo:hi] < waves - pair
        zero = jnp.zeros_like(mixed)
        both = jnp.concatenate(
            [jnp.where(keep, mixed, zero), jnp.where(keep, zero, mixed)], axis=0
        )
        both = dot(both, leg_s[(t - 1) % depth, i, lo:hi, :])
        half_rows = spec.shape[0]
        first = both[:half_rows] + dot(spec[:, :lo], leg_s[(t - 1) % depth, i, :lo, :])
        second = both[half_rows:]
        if not early:
            second = second + dot(spec[:, hi:], leg_s[(t - 1) % depth, i, hi:, :])
        parts = (first, second)
        for h in range(2):
            j = 2 * i + h
            main_s[pl.ds(j, rows, stride=8), :] = jnp.transpose(parts[h][:LANES])
            rest_s[step, 16 * j : 16 * j + 16, :] = parts[h][LANES:]

    def emit():
        out_ref[...] = main_s[...].reshape(dests, 32, LANES).astype(BF16)

    @pl.when(t == 0)
    def _():
        for step in range(depth):
            fetch(step).start()
        spread = spread_ref[:, var_ref[0], :]
        spread_s[:, waves:] = jnp.zeros((modes, spread_s.shape[1] - waves), F32)
        spread_s[:, :waves] = spread
        second_s[:, :waves] = pltpu.roll(spread, 1, 1)
        second_s[:, waves : waves + 1] = spread[:, waves - 1 :]
        wide_s[...] = vert_ref[...].astype(F32)
        vert = wide_s[:, var_ref[0], :]
        vert_s[...] = jnp.zeros_like(vert_s)
        vert_s[:modes, :] = vert.astype(BF16)
        rem_s[...] = jnp.zeros_like(rem_s)
        align(0)
        for i in range(4):
            scale(0, i)

    @pl.when((t > 0) & (t <= steps))
    def _():
        fetch(t - 1).wait()

    @pl.when((t > 1) & (t - 2 + depth < steps))
    def _():
        fetch(t - 2 + depth).start()

    for early in (True, False):

        @pl.when((t > 0) & (t <= steps) & ((base_ref[0] + 4 * t <= 128) == early))
        def _():
            emit()
            align(jnp.minimum(t, steps - 1))
            for i in range(4):
                sums(t - 1, i, early)
                scale(jnp.minimum(t, steps - 1), i)

    @pl.when(t == steps + 1)
    def _():
        emit()

    @pl.when(t == steps + 2)
    def _():
        for k in range(8 * steps):
            at = LANES * (k // GROUP) + REST * (k % GROUP)
            lo = 16 * (k % 8)
            rem_s[at : at + REST, :] = rest_s[k // 8, lo : lo + REST, :]
        for u in range(4):
            main_s[pl.ds(u, rows, stride=4), :] = jnp.transpose(rem_s[u * LANES : (u + 1) * LANES])
        out_ref[:, :16, :] = main_s[: 4 * rows, :].reshape(dests, 16, LANES).astype(BF16)


def fourier_blocks(control, spread, vertical, legendre, base, var, dests):
    pairs, slots, _, modes = control.shape
    rows = legendre.shape[2]
    ctrl = jnp.transpose(control, (0, 2, 3, 1))
    steps = pairs // 4
    return pl.pallas_call(
        fourier_kernel,
        out_shape=jax.ShapeDtypeStruct((dests, 32 * steps + 16, LANES), BF16),
        grid=(steps + 3,),
        in_specs=[
            pl.BlockSpec(memory_space=pltpu.SMEM),
            pl.BlockSpec(memory_space=pltpu.SMEM),
            pl.BlockSpec((4, 1, modes, slots), lambda t: (jnp.minimum(t, steps - 1), 0, 0, 0)),
            pl.BlockSpec((modes, 4, slots - 1), lambda t: (0, 0, 0)),
            pl.BlockSpec((modes, 4, modes), lambda t: (0, 0, 0)),
            pl.BlockSpec(memory_space=pl.ANY),
        ],
        out_specs=pl.BlockSpec((dests, 32, LANES), lambda t: (0, jnp.maximum(t - 2, 0), 0)),
        scratch_shapes=[
            pltpu.VMEM((rows * 8, LANES), F32),
            pltpu.VMEM((steps, LANES, rows), F32),
            pltpu.VMEM((4 * LANES, rows), F32),
            pltpu.VMEM((3, 4, slots, rows), BF16),
            pltpu.SemaphoreType.DMA((3,)),
            pltpu.VMEM((modes, 9 * LANES), F32),
            pltpu.VMEM((modes, 6 * LANES), F32),
            pltpu.VMEM((modes, 6 * LANES), F32),
            pltpu.VMEM((modes, 6 * LANES), BF16),
            pltpu.VMEM((4, 144, slots), BF16),
            pltpu.VMEM((144, modes), BF16),
            pltpu.VMEM((modes, 4, modes), F32),
        ],
        name="fourier",
    )(
        base,
        var,
        ctrl,
        jnp.transpose(spread, (2, 0, 1)),
        jnp.transpose(vertical, (1, 0, 2)),
        legendre,
    )


def cosine(turns):
    x = turns * math.pi
    y = x * x
    s = -1.0 / 39916800.0
    for c in (1.0 / 362880.0, -1.0 / 5040.0, 1.0 / 120.0, -1.0 / 6.0, 1.0):
        s = s * y + c
    s = s * x
    return 1.0 - 2.0 * (s * s)


def table_kernel(slots, index_ref, owner_ref, main_ref, row_ref, spot_ref):
    cols = index_ref.shape[1]
    depth = main_ref.shape[1]
    waves = depth // 2
    column = jnp.transpose(jnp.broadcast_to(index_ref[...].astype(F32), (LANES, cols)))
    row = jnp.floor((column + 0.5) * (1.0 / NLON))
    row_ref[...] = row
    column = column[:, :1]
    row = row[:, :1]
    longitude = column - row * NLON
    lane = lax.broadcasted_iota(jnp.int32, (1, depth), 1)

    source = lane // 80
    part = lane % 80 // 40
    local = lane % 40
    pair = source * 20 + local // 2
    wave = jnp.where(local % 2 == 0, pair, waves - 1 - pair)
    weight = jnp.where(wave == 0, 1.0, 2.0).astype(F32)
    wave_f = wave.astype(F32)
    shift = part.astype(F32) * (NLON // 4)
    for c in range(0, cols, 64):
        turns = longitude[c : c + 64] * wave_f + shift
        turns = turns - jnp.floor(turns * (1.0 / NLON) + 0.5) * NLON
        main_ref[c : c + 64, :] = (weight * cosine(turns * (1.0 / NLON))).astype(BF16)

    hits = lax.broadcasted_iota(jnp.int32, (LANES, cols), 0) == owner_ref[...]
    hits_f = jnp.where(hits, 1.0, 0.0).astype(F32)
    before = (
        lax.broadcasted_iota(jnp.int32, (cols, cols), 0)
        < lax.broadcasted_iota(jnp.int32, (cols, cols), 1)
    )
    earlier = dot(hits_f.astype(BF16), jnp.where(before, 1.0, 0.0).astype(BF16))
    first = (lax.broadcasted_iota(jnp.int32, (LANES, cols), 0) * slots).astype(F32)
    spot = jnp.sum(hits_f * (first + earlier), axis=0, keepdims=True).astype(jnp.int32)
    spot_ref[...] = spot


def tables(index, owner, depth, slots):
    cols = index.shape[1]
    return pl.pallas_call(
        functools.partial(table_kernel, slots),
        out_shape=(
            jax.ShapeDtypeStruct((cols, depth), BF16),
            jax.ShapeDtypeStruct((cols, LANES), F32),
            jax.ShapeDtypeStruct((1, cols), jnp.int32),
        ),
        cost_estimate=pl.CostEstimate(
            flops=60 * cols * depth, bytes_accessed=4 << 20, transcendentals=0
        ),
        compiler_params=pltpu.CompilerParams(vmem_limit_bytes=24 << 20),
        name="tables",
    )(index, owner)


def state_kernel(
    main_ref, spot_ref, row_ref, coeff_ref, out_ref, coeff_s, tail_s, take_s, state_s
):
    v = pl.program_id(0)
    cols = main_ref.shape[0]
    depth = main_ref.shape[1]
    sources = coeff_ref.shape[0]
    block = coeff_ref[...].astype(F32).reshape(sources * 2, 22, 8, LANES)
    for r in range(4):
        picked = jnp.stack([block[:, 4 * g + r] for g in range(5)], axis=1)
        coeff_s[:, r * LANES : (r + 1) * LANES] = picked.reshape(depth, LANES).astype(BF16)
    take_s[...] = block[:, 20:].reshape(sources * 2 * 16, LANES)
    lane = lax.broadcasted_iota(jnp.int32, (1, LANES), 1)
    odd = v % 2
    for u in range(4):
        picked = [take_s[pl.ds(4 * r + u, sources * 2, stride=16), :] for r in range(4)]
        for k in range(GROUP):
            at = pl.ds(v // 2 * depth + u * GROUP + k, sources * 2, stride=4 * GROUP)
            kept = tail_s[at, :]
            for r in range(4):
                moved = pltpu.roll(picked[r], (64 * odd + 16 * r - REST * k + LANES) % LANES, 1)
                kept = jnp.where(lane // 16 == 4 * odd + r, moved, kept)
            tail_s[at, :] = kept
    row = row_ref[...]
    products = dot(main_ref[...], coeff_s[...])
    main = products[:, :LANES]
    for r in range(1, 4):
        main = jnp.where(row == r, products[:, r * LANES : (r + 1) * LANES], main)
    state_s[:, pl.ds(pl.multiple_of(v * LANES, LANES), LANES)] = main.astype(BF16)

    @pl.when(v == pl.num_programs(0) - 1)
    def _():
        wide = jnp.concatenate([tail_s[:depth], tail_s[depth:]], axis=1)
        products = dot(main_ref[...], wide.astype(BF16))
        folded = []
        for half in range(2):
            part = products[:, half * LANES : (half + 1) * LANES]
            part = jnp.where((lane // 16 % 4).astype(F32) == row, part, 0.0)
            part = part + pltpu.roll(part, LANES - 32, 1)
            folded.append(part + pltpu.roll(part, LANES - 16, 1))
        tail = jnp.where(lane % 64 < 32, folded[0], pltpu.roll(folded[1], 32, 1))
        state_s[:, 4 * LANES :] = jnp.where(lane % 32 < 9, tail, 0.0).astype(BF16)
        place = lax.broadcasted_iota(jnp.int32, (out_ref.shape[0], cols), 0) == spot_ref[...]
        place = jnp.where(place, 1.0, 0.0).astype(BF16)
        out_ref[...] = dot(place, state_s[...]).astype(BF16)


def column_states(coeff, main_table, spot, row, slots):
    sources, rows, _ = coeff.shape
    cols, depth = main_table.shape
    total = slots * LANES
    whole = pl.BlockSpec(memory_space=pltpu.VMEM)
    return pl.pallas_call(
        state_kernel,
        out_shape=jax.ShapeDtypeStruct((total, 5 * LANES), BF16),
        grid=(4,),
        in_specs=[
            whole,
            whole,
            whole,
            pl.BlockSpec((sources, rows // 4, LANES), lambda v: (0, v, 0)),
        ],
        out_specs=whole,
        scratch_shapes=[
            pltpu.VMEM((depth, 4 * LANES), BF16),
            pltpu.VMEM((2 * depth, LANES), F32),
            pltpu.VMEM((sources * 2 * 16, LANES), F32),
            pltpu.VMEM((cols, 5 * LANES), BF16),
        ],
        compiler_params=pltpu.CompilerParams(vmem_limit_bytes=28 << 20),
        name="states",
    )(main_table, spot, row, coeff)


def answer_kernel(state_ref, jac_ref, bias_ref, out_ref, jac_s):
    channels = jac_ref.shape[1]
    levels = jac_ref.shape[0] // 4
    rest = levels - LANES

    jac = jac_ref[...].astype(F32)
    jac_s[...] = jnp.zeros_like(jac_s)
    for v in range(4):
        at = v * levels
        jac_s[v * LANES : (v + 1) * LANES, :] = jac[at : at + LANES].astype(BF16)
        lo = 4 * LANES + (v % 2 * 2 + v // 2) * SLOT_LANES
        piece = jnp.concatenate(
            [jac[at + LANES : at + levels], jnp.zeros((16 - rest, channels), F32)], axis=0
        )
        jac_s[lo : lo + 16, :] = piece.astype(BF16)

    total = state_ref.shape[0]
    for lo in range(0, total, total // 2):
        rows = slice(lo, lo + total // 2)
        depart = dot(state_ref[rows, :], jac_s[...]) + bias_ref[...]
        weighted = (depart / jnp.sqrt(1.0 + depart * depart * 0.25)).astype(BF16)
        out_ref[rows, :channels] = depart.astype(BF16)
        out_ref[rows, 3 * LANES : 3 * LANES + jac_ref.shape[0]] = lax.dot_general(
            weighted, jac_ref[...], (((1,), (1,)), ((), ())), preferred_element_type=F32
        ).astype(BF16)


def answers(states, jac_t, bias):
    total, lanes = states.shape
    width, channels = jac_t.shape
    out_lanes = -(-channels // LANES) * LANES + -(-width // LANES) * LANES
    return pl.pallas_call(
        answer_kernel,
        out_shape=jax.ShapeDtypeStruct((total, out_lanes), BF16),
        scratch_shapes=[pltpu.VMEM((lanes, channels), BF16)],
        compiler_params=pltpu.CompilerParams(vmem_limit_bytes=20 << 20),
        name="answers",
    )(states, jac_t, bias)


def collect_kernel(spot_ref, back_ref, depart_ref, grad_ref):
    cols = spot_ref.shape[1]
    total = back_ref.shape[0]
    spot = jnp.transpose(jnp.broadcast_to(spot_ref[...].astype(F32), (LANES, cols)))[:, :1]
    place = lax.broadcasted_iota(jnp.int32, (cols, total), 1) == spot.astype(jnp.int32)
    place = jnp.where(place, 1.0, 0.0).astype(BF16)
    channels = depart_ref.shape[0]
    width = grad_ref.shape[0]
    both = jnp.transpose(dot(place, back_ref[...]))
    depart_ref[...] = both[:channels].astype(BF16)
    grad_ref[...] = both[3 * LANES : 3 * LANES + width].astype(BF16)


def collect(spot, back, channels, width):
    cols = spot.shape[1]
    return pl.pallas_call(
        collect_kernel,
        out_shape=(
            jax.ShapeDtypeStruct((channels, cols), BF16),
            jax.ShapeDtypeStruct((width, cols), BF16),
        ),
        compiler_params=pltpu.CompilerParams(vmem_limit_bytes=20 << 20),
        name="collect",
    )(spot, back)


def exchange(x):
    return lax.all_to_all(x, ("wave", "lat"), split_axis=0, concat_axis=0, tiled=True)


def local(control, spread, vertical, legendre, column_index, column_owner, jacobian, channel_bias):
    pairs = control.shape[0]
    wave_count = lax.axis_size("wave")
    device_count = wave_count * lax.axis_size("lat")
    cols = column_index.shape[0]
    slots = max(2, 2 * cols // device_count)
    base = (lax.axis_index("wave") * pairs).astype(jnp.int32).reshape(1)
    var = (lax.axis_index("lat") // 2).astype(jnp.int32).reshape(1)
    blocks = fourier_blocks(control, spread, vertical, legendre, base, var, device_count)
    index = column_index.reshape(1, cols)
    main_table, row, spot = tables(
        index, column_owner.reshape(1, cols), 4 * pairs * wave_count, slots
    )
    coeff = exchange(blocks).reshape(wave_count, -1, LANES)
    outgoing = column_states(coeff, main_table, spot, row, slots)
    lanes = outgoing.shape[1]
    states = exchange(outgoing.reshape(device_count, slots, lanes))
    jac_t = jnp.transpose(jacobian[0])
    reply = answers(states.reshape(device_count * slots, lanes), jac_t, channel_bias)
    back = exchange(reply.reshape(device_count, slots, reply.shape[1]))
    departures, increments = collect(
        spot, back.reshape(device_count * slots, -1), jac_t.shape[1], jac_t.shape[0]
    )
    return (jnp.transpose(departures), jnp.transpose(increments))


def solution(mesh):
    return jax.shard_map(
        local,
        mesh=mesh,
        in_specs=(
            P("wave", None, "lat", None),
            P(),
            P(),
            P("wave", None, None),
            P(("wave", "lat")),
            P(("wave", "lat"), None),
            P(("wave", "lat"), None, None),
            P(("wave", "lat"), None),
        ),
        out_specs=(P(("wave", "lat"), None), P(("wave", "lat"), None)),
        check_vma=False,
    )
```

```python
import functools
import math

import jax
import jax.numpy as jnp
from jax import lax
from jax.experimental import pallas as pl
from jax.experimental.pallas import tpu as pltpu
from jax.sharding import PartitionSpec as P

NLON = 2560
LANES = 128
SLOT_LANES = 32
REST = 12
GROUP = 10
F32 = jnp.float32
BF16 = jnp.bfloat16


def dot(a, b):
    return jnp.dot(a, b, preferred_element_type=F32)


def fourier_kernel(
    base_ref,
    var_ref,
    ctrl_ref,
    spread_ref,
    vert_ref,
    leg_ref,
    out_ref,
    main_s,
    rest_s,
    rem_s,
    leg_s,
    leg_sem,
    spread_s,
    second_s,
    first_s,
    scaled_s,
    spec_s,
    vert_s,
    wide_s,
):
    slots = ctrl_ref.shape[3]
    waves = slots - 1
    modes = ctrl_ref.shape[2]
    rows = leg_ref.shape[2]
    dests = out_ref.shape[0]
    steps = pl.num_programs(0) - 3
    depth = leg_s.shape[0]
    t = pl.program_id(0)
    lane = lax.broadcasted_iota(jnp.int32, (1, LANES), 1)
    slot = lax.broadcasted_iota(jnp.int32, (1, slots), 1)

    def fetch(step):
        at = step % depth
        return pltpu.make_async_copy(
            leg_ref.at[pl.ds(4 * step, 4)], leg_s.at[at], leg_sem.at[at]
        )

    def align(step):
        pair = base_ref[0] + step * 4
        skip = pair // LANES
        shift = pair - skip * LANES
        last = None
        for k in range(6):
            if last is None:
                last = pltpu.roll(
                    spread_s[:, pl.ds(pl.multiple_of(skip * LANES, LANES), LANES)], LANES - shift, 1
                )
            after = spread_s[:, pl.ds(pl.multiple_of((skip + k + 1) * LANES, LANES), LANES)]
            after = pltpu.roll(after, LANES - shift, 1)
            first_s[:, k * LANES : (k + 1) * LANES] = jnp.where(lane < LANES - shift, last, after)
            last = after

    def scale(step, i):
        pair = base_ref[0] + step * 4 + i
        last = first_s[:, :LANES]
        last = pltpu.roll(last, LANES - i, 1) if i else last
        for k in range(5):
            at = slice(k * LANES, (k + 1) * LANES)
            after = first_s[:, (k + 1) * LANES : (k + 2) * LANES]
            after = pltpu.roll(after, LANES - i, 1) if i else after
            factor = jnp.where(lane < LANES - i, last, after) if i else last
            last = after
            if k >= 2:
                factor = jnp.where(lane + k * LANES < waves - pair, factor, second_s[:, at])
            scaled_s[:, at] = (ctrl_ref[i, 0, :, at].astype(F32) * factor).astype(BF16)
        end = ctrl_ref[i, 0, :, waves:].astype(F32) * second_s[:, waves : waves + 1]
        scaled_s[:, waves : waves + 1] = end.astype(BF16)
        spec_s[i] = dot(vert_s[...], scaled_s[:, :slots]).astype(BF16)

    def sums(step, i, early):
        pair = base_ref[0] + step * 4 + i
        spec = spec_s[i]
        lo, hi = (512, slots) if early else (256, 512)
        mixed = spec[:, lo:hi]
        keep = slot[:, lo:hi] < waves - pair
        zero = jnp.zeros_like(mixed)
        both = jnp.concatenate(
            [jnp.where(keep, mixed, zero), jnp.where(keep, zero, mixed)], axis=0
        )
        both = dot(both, leg_s[(t - 1) % depth, i, lo:hi, :])
        half_rows = spec.shape[0]
        first = both[:half_rows] + dot(spec[:, :lo], leg_s[(t - 1) % depth, i, :lo, :])
        second = both[half_rows:]
        if not early:
            second = second + dot(spec[:, hi:], leg_s[(t - 1) % depth, i, hi:, :])
        parts = (first, second)
        for h in range(2):
            j = 2 * i + h
            main_s[pl.ds(j, rows, stride=8), :] = jnp.transpose(parts[h][:LANES])
            rest_s[step, 16 * j : 16 * j + 16, :] = parts[h][LANES:]

    def emit():
        out_ref[...] = main_s[...].reshape(dests, 32, LANES).astype(BF16)

    @pl.when(t == 0)
    def _():
        for step in range(depth):
            fetch(step).start()
        spread = spread_ref[:, var_ref[0], :]
        spread_s[:, waves:] = jnp.zeros((modes, spread_s.shape[1] - waves), F32)
        spread_s[:, :waves] = spread
        second_s[:, :waves] = pltpu.roll(spread, 1, 1)
        second_s[:, waves : waves + 1] = spread[:, waves - 1 :]
        wide_s[...] = vert_ref[...].astype(F32)
        vert = wide_s[:, var_ref[0], :]
        vert_s[...] = jnp.zeros_like(vert_s)
        vert_s[:modes, :] = vert.astype(BF16)
        rem_s[...] = jnp.zeros_like(rem_s)
        align(0)
        for i in range(4):
            scale(0, i)

    @pl.when((t > 0) & (t <= steps))
    def _():
        fetch(t - 1).wait()

    @pl.when((t > 1) & (t - 2 + depth < steps))
    def _():
        fetch(t - 2 + depth).start()

    for early in (True, False):

        @pl.when((t > 0) & (t <= steps) & ((base_ref[0] + 4 * t <= 128) == early))
        def _():
            emit()
            align(jnp.minimum(t, steps - 1))
            for i in range(4):
                sums(t - 1, i, early)
                scale(jnp.minimum(t, steps - 1), i)

    @pl.when(t == steps + 1)
    def _():
        emit()

    @pl.when(t == steps + 2)
    def _():
        for k in range(8 * steps):
            at = LANES * (k // GROUP) + REST * (k % GROUP)
            lo = 16 * (k % 8)
            rem_s[at : at + REST, :] = rest_s[k // 8, lo : lo + REST, :]
        for u in range(4):
            main_s[pl.ds(u, rows, stride=4), :] = jnp.transpose(rem_s[u * LANES : (u + 1) * LANES])
        out_ref[:, :16, :] = main_s[: 4 * rows, :].reshape(dests, 16, LANES).astype(BF16)


def fourier_blocks(control, spread, vertical, legendre, base, var, dests):
    pairs, slots, _, modes = control.shape
    rows = legendre.shape[2]
    ctrl = jnp.transpose(control, (0, 2, 3, 1))
    steps = pairs // 4
    return pl.pallas_call(
        fourier_kernel,
        out_shape=jax.ShapeDtypeStruct((dests, 32 * steps + 16, LANES), BF16),
        grid=(steps + 3,),
        in_specs=[
            pl.BlockSpec(memory_space=pltpu.SMEM),
            pl.BlockSpec(memory_space=pltpu.SMEM),
            pl.BlockSpec((4, 1, modes, slots), lambda t: (jnp.minimum(t, steps - 1), 0, 0, 0)),
            pl.BlockSpec((modes, 4, slots - 1), lambda t: (0, 0, 0)),
            pl.BlockSpec((modes, 4, modes), lambda t: (0, 0, 0)),
            pl.BlockSpec(memory_space=pl.ANY),
        ],
        out_specs=pl.BlockSpec((dests, 32, LANES), lambda t: (0, jnp.maximum(t - 2, 0), 0)),
        scratch_shapes=[
            pltpu.VMEM((rows * 8, LANES), F32),
            pltpu.VMEM((steps, LANES, rows), F32),
            pltpu.VMEM((4 * LANES, rows), F32),
            pltpu.VMEM((steps, 4, slots, rows), BF16),
            pltpu.SemaphoreType.DMA((steps,)),
            pltpu.VMEM((modes, 9 * LANES), F32),
            pltpu.VMEM((modes, 6 * LANES), F32),
            pltpu.VMEM((modes, 6 * LANES), F32),
            pltpu.VMEM((modes, 6 * LANES), BF16),
            pltpu.VMEM((4, 144, slots), BF16),
            pltpu.VMEM((144, modes), BF16),
            pltpu.VMEM((modes, 4, modes), F32),
        ],
        name="fourier",
    )(
        base,
        var,
        ctrl,
        jnp.transpose(spread, (2, 0, 1)),
        jnp.transpose(vertical, (1, 0, 2)),
        legendre,
    )


def cosine(turns):
    x = turns * math.pi
    y = x * x
    s = -1.0 / 39916800.0
    for c in (1.0 / 362880.0, -1.0 / 5040.0, 1.0 / 120.0, -1.0 / 6.0, 1.0):
        s = s * y + c
    s = s * x
    return 1.0 - 2.0 * (s * s)


def table_kernel(slots, index_ref, owner_ref, main_ref, row_ref, spot_ref):
    cols = index_ref.shape[1]
    depth = main_ref.shape[1]
    waves = depth // 2
    column = jnp.transpose(jnp.broadcast_to(index_ref[...].astype(F32), (LANES, cols)))
    row = jnp.floor((column + 0.5) * (1.0 / NLON))
    row_ref[...] = row
    column = column[:, :1]
    row = row[:, :1]
    longitude = column - row * NLON
    lane = lax.broadcasted_iota(jnp.int32, (1, depth), 1)

    source = lane // 80
    part = lane % 80 // 40
    local = lane % 40
    pair = source * 20 + local // 2
    wave = jnp.where(local % 2 == 0, pair, waves - 1 - pair)
    weight = jnp.where(wave == 0, 1.0, 2.0).astype(F32)
    wave_f = wave.astype(F32)
    shift = part.astype(F32) * (NLON // 4)
    for c in range(0, cols, 64):
        turns = longitude[c : c + 64] * wave_f + shift
        turns = turns - jnp.floor(turns * (1.0 / NLON) + 0.5) * NLON
        main_ref[c : c + 64, :] = (weight * cosine(turns * (1.0 / NLON))).astype(BF16)

    hits = lax.broadcasted_iota(jnp.int32, (LANES, cols), 0) == owner_ref[...]
    hits_f = jnp.where(hits, 1.0, 0.0).astype(F32)
    before = (
        lax.broadcasted_iota(jnp.int32, (cols, cols), 0)
        < lax.broadcasted_iota(jnp.int32, (cols, cols), 1)
    )
    earlier = dot(hits_f.astype(BF16), jnp.where(before, 1.0, 0.0).astype(BF16))
    first = (lax.broadcasted_iota(jnp.int32, (LANES, cols), 0) * slots).astype(F32)
    spot = jnp.sum(hits_f * (first + earlier), axis=0, keepdims=True).astype(jnp.int32)
    spot_ref[...] = spot


def tables(index, owner, depth, slots):
    cols = index.shape[1]
    return pl.pallas_call(
        functools.partial(table_kernel, slots),
        out_shape=(
            jax.ShapeDtypeStruct((cols, depth), BF16),
            jax.ShapeDtypeStruct((cols, LANES), F32),
            jax.ShapeDtypeStruct((1, cols), jnp.int32),
        ),
        cost_estimate=pl.CostEstimate(
            flops=60 * cols * depth, bytes_accessed=4 << 20, transcendentals=0
        ),
        compiler_params=pltpu.CompilerParams(vmem_limit_bytes=24 << 20),
        name="tables",
    )(index, owner)


def state_kernel(
    main_ref, spot_ref, row_ref, coeff_ref, out_ref, coeff_s, tail_s, take_s, state_s
):
    v = pl.program_id(0)
    cols = main_ref.shape[0]
    depth = main_ref.shape[1]
    sources = coeff_ref.shape[0]
    block = coeff_ref[...].astype(F32).reshape(sources * 2, 22, 8, LANES)
    for r in range(4):
        picked = jnp.stack([block[:, 4 * g + r] for g in range(5)], axis=1)
        coeff_s[:, r * LANES : (r + 1) * LANES] = picked.reshape(depth, LANES).astype(BF16)
    take_s[...] = block[:, 20:].reshape(sources * 2 * 16, LANES)
    lane = lax.broadcasted_iota(jnp.int32, (1, LANES), 1)
    odd = v % 2
    for u in range(4):
        picked = [take_s[pl.ds(4 * r + u, sources * 2, stride=16), :] for r in range(4)]
        for k in range(GROUP):
            at = pl.ds(v // 2 * depth + u * GROUP + k, sources * 2, stride=4 * GROUP)
            kept = tail_s[at, :]
            for r in range(4):
                moved = pltpu.roll(picked[r], (64 * odd + 16 * r - REST * k + LANES) % LANES, 1)
                kept = jnp.where(lane // 16 == 4 * odd + r, moved, kept)
            tail_s[at, :] = kept
    row = row_ref[...]
    products = dot(main_ref[...], coeff_s[...])
    main = products[:, :LANES]
    for r in range(1, 4):
        main = jnp.where(row == r, products[:, r * LANES : (r + 1) * LANES], main)
    state_s[:, pl.ds(pl.multiple_of(v * LANES, LANES), LANES)] = main.astype(BF16)

    @pl.when(v == pl.num_programs(0) - 1)
    def _():
        wide = jnp.concatenate([tail_s[:depth], tail_s[depth:]], axis=1)
        products = dot(main_ref[...], wide.astype(BF16))
        folded = []
        for half in range(2):
            part = products[:, half * LANES : (half + 1) * LANES]
            part = jnp.where((lane // 16 % 4).astype(F32) == row, part, 0.0)
            part = part + pltpu.roll(part, LANES - 32, 1)
            folded.append(part + pltpu.roll(part, LANES - 16, 1))
        tail = jnp.where(lane % 64 < 32, folded[0], pltpu.roll(folded[1], 32, 1))
        state_s[:, 4 * LANES :] = jnp.where(lane % 32 < 9, tail, 0.0).astype(BF16)
        place = lax.broadcasted_iota(jnp.int32, (out_ref.shape[0], cols), 0) == spot_ref[...]
        place = jnp.where(place, 1.0, 0.0).astype(BF16)
        out_ref[...] = dot(place, state_s[...]).astype(BF16)


def column_states(coeff, main_table, spot, row, slots):
    sources, rows, _ = coeff.shape
    cols, depth = main_table.shape
    total = slots * LANES
    whole = pl.BlockSpec(memory_space=pltpu.VMEM)
    return pl.pallas_call(
        state_kernel,
        out_shape=jax.ShapeDtypeStruct((total, 5 * LANES), BF16),
        grid=(4,),
        in_specs=[
            whole,
            whole,
            whole,
            pl.BlockSpec((sources, rows // 4, LANES), lambda v: (0, v, 0)),
        ],
        out_specs=whole,
        scratch_shapes=[
            pltpu.VMEM((depth, 4 * LANES), BF16),
            pltpu.VMEM((2 * depth, LANES), F32),
            pltpu.VMEM((sources * 2 * 16, LANES), F32),
            pltpu.VMEM((cols, 5 * LANES), BF16),
        ],
        compiler_params=pltpu.CompilerParams(vmem_limit_bytes=28 << 20),
        name="states",
    )(main_table, spot, row, coeff)


def answer_kernel(state_ref, jac_ref, bias_ref, out_ref, jac_s):
    channels = jac_ref.shape[1]
    levels = jac_ref.shape[0] // 4
    rest = levels - LANES

    jac = jac_ref[...].astype(F32)
    jac_s[...] = jnp.zeros_like(jac_s)
    for v in range(4):
        at = v * levels
        jac_s[v * LANES : (v + 1) * LANES, :] = jac[at : at + LANES].astype(BF16)
        lo = 4 * LANES + (v % 2 * 2 + v // 2) * SLOT_LANES
        piece = jnp.concatenate(
            [jac[at + LANES : at + levels], jnp.zeros((16 - rest, channels), F32)], axis=0
        )
        jac_s[lo : lo + 16, :] = piece.astype(BF16)

    total = state_ref.shape[0]
    for lo in range(0, total, total // 2):
        rows = slice(lo, lo + total // 2)
        depart = dot(state_ref[rows, :], jac_s[...]) + bias_ref[...]
        weighted = (depart / jnp.sqrt(1.0 + depart * depart * 0.25)).astype(BF16)
        out_ref[rows, :channels] = depart.astype(BF16)
        out_ref[rows, 3 * LANES : 3 * LANES + jac_ref.shape[0]] = lax.dot_general(
            weighted, jac_ref[...], (((1,), (1,)), ((), ())), preferred_element_type=F32
        ).astype(BF16)


def answers(states, jac_t, bias):
    total, lanes = states.shape
    width, channels = jac_t.shape
    out_lanes = -(-channels // LANES) * LANES + -(-width // LANES) * LANES
    return pl.pallas_call(
        answer_kernel,
        out_shape=jax.ShapeDtypeStruct((total, out_lanes), BF16),
        scratch_shapes=[pltpu.VMEM((lanes, channels), BF16)],
        compiler_params=pltpu.CompilerParams(vmem_limit_bytes=20 << 20),
        name="answers",
    )(states, jac_t, bias)


def collect_kernel(spot_ref, back_ref, depart_ref, grad_ref):
    cols = spot_ref.shape[1]
    total = back_ref.shape[0]
    spot = jnp.transpose(jnp.broadcast_to(spot_ref[...].astype(F32), (LANES, cols)))[:, :1]
    place = lax.broadcasted_iota(jnp.int32, (cols, total), 1) == spot.astype(jnp.int32)
    place = jnp.where(place, 1.0, 0.0).astype(BF16)
    channels = depart_ref.shape[0]
    width = grad_ref.shape[0]
    both = jnp.transpose(dot(place, back_ref[...]))
    depart_ref[...] = both[:channels].astype(BF16)
    grad_ref[...] = both[3 * LANES : 3 * LANES + width].astype(BF16)


def collect(spot, back, channels, width):
    cols = spot.shape[1]
    return pl.pallas_call(
        collect_kernel,
        out_shape=(
            jax.ShapeDtypeStruct((channels, cols), BF16),
            jax.ShapeDtypeStruct((width, cols), BF16),
        ),
        compiler_params=pltpu.CompilerParams(vmem_limit_bytes=20 << 20),
        name="collect",
    )(spot, back)


def exchange(x):
    return lax.all_to_all(x, ("wave", "lat"), split_axis=0, concat_axis=0, tiled=True)


def local(control, spread, vertical, legendre, column_index, column_owner, jacobian, channel_bias):
    pairs = control.shape[0]
    wave_count = lax.axis_size("wave")
    device_count = wave_count * lax.axis_size("lat")
    cols = column_index.shape[0]
    slots = max(2, 2 * cols // device_count)
    base = (lax.axis_index("wave") * pairs).astype(jnp.int32).reshape(1)
    var = (lax.axis_index("lat") // 2).astype(jnp.int32).reshape(1)
    blocks = fourier_blocks(control, spread, vertical, legendre, base, var, device_count)
    index = column_index.reshape(1, cols)
    main_table, row, spot = tables(
        index, column_owner.reshape(1, cols), 4 * pairs * wave_count, slots
    )
    coeff = exchange(blocks).reshape(wave_count, -1, LANES)
    outgoing = column_states(coeff, main_table, spot, row, slots)
    lanes = outgoing.shape[1]
    states = exchange(outgoing.reshape(device_count, slots, lanes))
    jac_t = jnp.transpose(jacobian[0])
    reply = answers(states.reshape(device_count * slots, lanes), jac_t, channel_bias)
    back = exchange(reply.reshape(device_count, slots, reply.shape[1]))
    departures, increments = collect(
        spot, back.reshape(device_count * slots, -1), jac_t.shape[1], jac_t.shape[0]
    )
    return (jnp.transpose(departures), jnp.transpose(increments))


def solution(mesh):
    return jax.shard_map(
        local,
        mesh=mesh,
        in_specs=(
            P("wave", None, "lat", None),
            P(),
            P(),
            P("wave", None, None),
            P(("wave", "lat")),
            P(("wave", "lat"), None),
            P(("wave", "lat"), None, None),
            P(("wave", "lat"), None),
        ),
        out_specs=(P(("wave", "lat"), None), P(("wave", "lat"), None)),
        check_vma=False,
    )
```
